128 devices in a mesh: row: 16 (over y, x_lo, core), col: 8 (over z, x_hi).
Axes of the slice: x: 4 (x_hi: 2, x_lo: 2; x = x_hi * 2 + x_lo), y: 4, z: 4, core: 2. Of those that a mesh axis runs over, the one named last changes fastest.
Arguments:
- homolog_activations: bfloat16 [256, 704, 256], P('row', 'col'), may hold values from -8 to 8
- coupling_activations: bfloat16 [704, 704, 128], P('row', 'col'), may hold values from -6 to 6
- homolog_existence_marks: int32 [256, 704], P('row', 'col'), may hold values from 0 to 1, as said below
- observed_peptide_marks: int32 [704], replicated, may hold values 0 or 1
- peptide_ordinals: int32 [704], replicated, may hold values from 1 to 2112, as said below
- strand_membership: int32 [704], replicated, may hold values from 0 to 7, never falling along the last dimension, each value on 1 to 176 neighbouring positions
- distance_ordinal_vectors: bfloat16 [66, 128], replicated, may hold values from -6 to 6
- coupling_score_mapping: bfloat16 [128, 8], replicated, may hold values from -0.5 to 0.5
- question_mapping_weights: bfloat16 [256, 256], replicated, may hold values from -4 to 4
- address_payload_mapping: bfloat16 [256, 512], replicated, may hold values from -4 to 4
- logistic_valve_mapping: bfloat16 [256, 256], replicated, may hold values from -0.375 to 0.375
- mixture_exit_mapping: bfloat16 [256, 256], replicated, may hold values from -0.375 to 0.375
- twofold_covariance_mapping: bfloat16 [256, 64], replicated, may hold values from -0.375 to 0.375
- covariance_exit_mapping: bfloat16 [1024, 128], replicated, may hold values from -0.1875 to 0.1875
- triad_opening_mappings: bfloat16 [128, 512], replicated, may hold values from -0.5 to 0.5
- triad_valve_mapping: bfloat16 [128, 128], replicated, may hold values from -0.5 to 0.5
- triad_exit_mapping: bfloat16 [128, 128], replicated, may hold values from -0.5 to 0.5
Outputs:
- homologs_after: bfloat16 [256, 704, 256], P('row', 'col')
- couplings_after: bfloat16 [704, 704, 128], P('row', 'col')
The draws below stay inside these ranges and needn't reach their ends.
Inputs may be any that keep to these rules, and one draw needn't show every extreme that they name: Row 0 and column 0 of homolog_existence_marks are all ones. `peptide_ordinals`: strictly increasing along the residues.
All inputs are finite; a program needn't handle non-finite values.
Results may differ from the reference program's by a relative error of at most 0.008.
Values may be sent and summed in bfloat16 or wider, within the bound.
A program may use at most 192 MiB of HBM per device.

```python
import math
import jax
import jax.numpy as jnp
import numpy as np
from jax import lax

ALIGNMENT_WIDTH = 256
PAIR_W = 128
ATTENTION_HEADS = 8
HEAD_CHANNELS = 32
OUTER_CHANNELS = 32
TRI_W = 128
REL_MAX = 32
RT = 44
SEQUENCE_COUNT = 256
RESIDUE_COUNT = 704
N_ROW = 16


def attention_tables(key):
    random_base_key = jax.random.fold_in(key, 202)
    matrix_shape = (ALIGNMENT_WIDTH, ATTENTION_HEADS, HEAD_CHANNELS)
    query_base = jax.random.normal(jax.random.fold_in(random_base_key, 1), matrix_shape, jnp.float32)
    key_extra = jax.random.normal(jax.random.fold_in(random_base_key, 2), matrix_shape, jnp.float32)
    value_base = jax.random.normal(jax.random.fold_in(random_base_key, 3), matrix_shape, jnp.float32)
    query_matrix = query_base
    key_matrix = key_extra
    scale_for_norm = 1.0 / math.sqrt(ALIGNMENT_WIDTH)
    return (query_matrix * scale_for_norm, key_matrix * scale_for_norm, value_base * scale_for_norm)


def draw_question_mapping_weights(key, part):
    query_matrix, key_matrix, value_matrix = attention_tables(key)
    return jnp.clip(query_matrix.reshape(ALIGNMENT_WIDTH, ATTENTION_HEADS * HEAD_CHANNELS), -4.0, 4.0).astype(jnp.bfloat16)


def draw_address_payload_mapping(key, part):
    query_matrix, key_matrix, value_matrix = attention_tables(key)
    joined_parts = jnp.concatenate([key_matrix.reshape(ALIGNMENT_WIDTH, ATTENTION_HEADS * HEAD_CHANNELS), value_matrix.reshape(ALIGNMENT_WIDTH, ATTENTION_HEADS * HEAD_CHANNELS)], axis=1)
    return jnp.clip(joined_parts, -4.0, 4.0).astype(jnp.bfloat16)


def draw_homolog_activations(key, part):
    random_base_key = jax.random.fold_in(key, 101)
    shared_values = jax.random.normal(jax.random.fold_in(random_base_key, 1), (RESIDUE_COUNT, ALIGNMENT_WIDTH), jnp.float32)
    random_offsets = jax.random.normal(jax.random.fold_in(random_base_key, 2), (SEQUENCE_COUNT, RESIDUE_COUNT, ALIGNMENT_WIDTH), jnp.float32)
    field = 0.7 * shared_values[None] + 0.7 * random_offsets
    return jnp.clip(field, -8.0, 8.0).astype(jnp.bfloat16)


def draw_homolog_existence_marks(key, part):
    rolls = jax.random.randint(jax.random.fold_in(key, 303), (SEQUENCE_COUNT, RESIDUE_COUNT), 0, 10 * SEQUENCE_COUNT)
    limit = 3 * SEQUENCE_COUNT + 6 * jnp.arange(SEQUENCE_COUNT, dtype=jnp.int32)[:, None]
    presence = (rolls < limit).astype(jnp.int32)
    presence = presence.at[0, :].set(1)
    presence = presence.at[:, 0].set(1)
    return presence


def draw_peptide_ordinals(key, part):
    gaps = jax.random.randint(jax.random.fold_in(key, 404), (RESIDUE_COUNT,), 1, 4)
    gaps = gaps.at[0].set(1)
    numbers = jnp.cumsum(gaps).astype(jnp.int32)
    numbers = numbers.at[RESIDUE_COUNT - 1].set(3 * RESIDUE_COUNT)
    return numbers.astype(jnp.int32)


def touch_ends(values, own_key, least, high):
    dims = values.shape
    place = [jax.random.randint(jax.random.fold_in(own_key, axis), (), 0, dims[axis]) for axis in range(len(dims))]
    values = values.at[tuple(place)].set(least)
    longest = dims.index(max(dims))
    place[longest] = (place[longest] + 1) % dims[longest]
    return values.at[tuple(place)].set(high)


def block_levels(key, dims, split, low, top_value):
    def one(dim, blocks):
        draws = jax.random.uniform(jax.random.fold_in(jax.random.fold_in(key, 6), dim), (blocks,), jnp.float32, low / len(split), top_value / len(split))
        return jnp.repeat(jnp.exp(draws), dims[dim] // blocks).reshape((-1,) + (1,) * (len(dims) - dim - 1))

    gain = one(*split[0])
    for cut in split[1:]:
        gain = gain * one(*cut)
    return gain


def length_profile(amount, total, bound, skew):
    weights = [(1 << 20) // math.isqrt(standing ** skew) + 1 for standing in range(2, amount + 1)]
    spare, given = total - bound - (amount - 1), [1] * (amount - 1)
    while spare > 0:
        movable = [i for i in range(amount - 1) if given[i] < bound]
        whole, budget = sum([weights[i] for i in movable]), spare
        for i in movable:
            extra = min(bound - given[i], max(1, budget * weights[i] // whole), spare)
            given[i] = given[i] + extra
            spare = spare - extra
    return np.array([bound] + given)


def uneven_parts(key, number_of, total, most, skew):
    if number_of == 2:
        one = jax.random.randint(key, (), max(1, total - most), min(most, total - 1) + 1)
        return jnp.stack([one, total - one])
    sizes = jnp.asarray(length_profile(number_of, total, most, skew), jnp.int32)
    twos = (number_of - 1) // 2
    source_of, receiver = sizes[1:1 + 2 * twos:2], sizes[2:2 + 2 * twos:2]
    room = jnp.minimum(source_of - 1, most - receiver)
    passed = jax.random.randint(jax.random.fold_in(key, 1), (twos,), 0, 1 << 20) % (room + 1)
    sizes = sizes.at[1:1 + 2 * twos:2].set(source_of - passed).at[2:2 + 2 * twos:2].set(receiver + passed)
    return sizes[jax.random.permutation(jax.random.fold_in(key, 2), number_of)]


def bell_draw(stream_key, extent, width, most, split=(), kind=jnp.bfloat16):
    gain = block_levels(stream_key, extent, split, -0.22, 0.18) if split else 1.0
    drawn = jax.random.normal(stream_key, extent, jnp.float32) * width * gain
    return jnp.minimum(jnp.maximum(drawn, -most), most).astype(kind)


def setup_inputs(seed: int = 0) -> dict:
    key_of = jax.random.split(jax.random.key(seed), 18)
    homolog_activations = draw_homolog_activations(jax.random.fold_in(key_of[17], 71), 0)
    coupling_activations = bell_draw(key_of[1], (RESIDUE_COUNT, RESIDUE_COUNT, PAIR_W), 1.0, 6.0, ((0, 16), (1, 8)))
    homolog_existence_marks = draw_homolog_existence_marks(jax.random.fold_in(key_of[17], 71), 0)
    observed_peptide_marks = touch_ends((jax.random.randint(key_of[3], (RESIDUE_COUNT,), 0, 4) < 3).astype(jnp.int32), jax.random.fold_in(key_of[3], 1), 0, 1)
    peptide_ordinals = draw_peptide_ordinals(jax.random.fold_in(key_of[17], 71), 0)
    strand_membership = jnp.searchsorted(jnp.cumsum(uneven_parts(key_of[5], 8, RESIDUE_COUNT, RESIDUE_COUNT // 4, 0)), jnp.arange(RESIDUE_COUNT), side="right").astype(jnp.int32)
    distance_ordinal_vectors = bell_draw(key_of[6], (2 * REL_MAX + 2, PAIR_W), 1.0, 6.0)
    coupling_score_mapping = bell_draw(key_of[7], (PAIR_W, ATTENTION_HEADS), PAIR_W ** -0.5, 0.5)
    question_mapping_weights = draw_question_mapping_weights(jax.random.fold_in(key_of[17], 71), 0)
    address_payload_mapping = draw_address_payload_mapping(jax.random.fold_in(key_of[17], 71), 0)
    logistic_valve_mapping = bell_draw(key_of[10], (ALIGNMENT_WIDTH, ATTENTION_HEADS * HEAD_CHANNELS), ALIGNMENT_WIDTH ** -0.5, 0.375)
    mixture_exit_mapping = bell_draw(key_of[11], (ATTENTION_HEADS * HEAD_CHANNELS, ALIGNMENT_WIDTH), (ATTENTION_HEADS * HEAD_CHANNELS) ** -0.5, 0.375)
    twofold_covariance_mapping = bell_draw(key_of[12], (ALIGNMENT_WIDTH, 2 * OUTER_CHANNELS), ALIGNMENT_WIDTH ** -0.5, 0.375)
    covariance_exit_mapping = bell_draw(key_of[13], (OUTER_CHANNELS * OUTER_CHANNELS, PAIR_W), (OUTER_CHANNELS * OUTER_CHANNELS) ** -0.5, 0.1875)
    triad_opening_mappings = bell_draw(key_of[14], (PAIR_W, 4 * TRI_W), PAIR_W ** -0.5, 0.5)
    triad_valve_mapping = bell_draw(key_of[15], (PAIR_W, PAIR_W), PAIR_W ** -0.5, 0.5)
    triad_exit_mapping = bell_draw(key_of[16], (TRI_W, PAIR_W), TRI_W ** -0.5, 0.5)
    return dict(homolog_activations=homolog_activations, coupling_activations=coupling_activations, homolog_existence_marks=homolog_existence_marks, observed_peptide_marks=observed_peptide_marks, peptide_ordinals=peptide_ordinals, strand_membership=strand_membership, distance_ordinal_vectors=distance_ordinal_vectors, coupling_score_mapping=coupling_score_mapping, question_mapping_weights=question_mapping_weights, address_payload_mapping=address_payload_mapping, logistic_valve_mapping=logistic_valve_mapping, mixture_exit_mapping=mixture_exit_mapping, twofold_covariance_mapping=twofold_covariance_mapping, covariance_exit_mapping=covariance_exit_mapping, triad_opening_mappings=triad_opening_mappings, triad_valve_mapping=triad_valve_mapping, triad_exit_mapping=triad_exit_mapping)


norm_eps = 1e-05
count_eps = 0.001
masked_score = -1000000000.0

def zscore_transform(inputs):
    inputs = inputs.astype(jnp.float32)
    centred = inputs - lax.optimization_barrier(jnp.mean(inputs, axis=-1, keepdims=True))
    spread = lax.optimization_barrier(jnp.mean(centred * centred, axis=-1, keepdims=True))
    return centred * lax.rsqrt(spread + norm_eps)

def regrouped_covariance(operand, weights):
    batch_shape = operand.shape[:-1]
    result = jnp.dot(operand.reshape(-1, operand.shape[-1]), weights, preferred_element_type=jnp.float32)
    return result.reshape(batch_shape + (weights.shape[-1],))

def quantized_numbers(tensor):
    return lax.optimization_barrier(tensor.astype(jnp.bfloat16)).astype(jnp.float32)

def position_bins(index_rows, index_cols, chain_rows, chain_cols):
    offset = jnp.clip(index_rows[:, None] - index_cols[None, :] + REL_MAX, 0, 2 * REL_MAX)
    return jnp.where(chain_rows[:, None] == chain_cols[None, :], offset, 2 * REL_MAX + 1).astype(jnp.int32)

def reference(homolog_activations, coupling_activations, homolog_existence_marks, observed_peptide_marks, peptide_ordinals, strand_membership, distance_ordinal_vectors, coupling_score_mapping, question_mapping_weights, address_payload_mapping, logistic_valve_mapping, mixture_exit_mapping, twofold_covariance_mapping, covariance_exit_mapping, triad_opening_mappings, triad_valve_mapping, triad_exit_mapping):
    similarity_breadth = ATTENTION_HEADS * HEAD_CHANNELS
    zscored_homologs = zscore_transform(homolog_activations).astype(jnp.bfloat16)
    existing_homolog_marks = homolog_existence_marks.astype(jnp.float32)
    covariance_source = quantized_numbers(regrouped_covariance(zscored_homologs, twofold_covariance_mapping) * existing_homolog_marks[:, :, None])
    left_all = covariance_source[:, :, :OUTER_CHANNELS]
    right_all = covariance_source[:, :, OUTER_CHANNELS:]
    counts = jnp.dot(existing_homolog_marks.T, existing_homolog_marks, precision=lax.Precision.HIGHEST)

    def opm_block(block_start):
        row_block = lax.dynamic_slice_in_dim(left_all, block_start, RT, 1)
        outer_prod = quantized_numbers(jnp.einsum('sic,sje->ijce', row_block, right_all))
        mixed_opm = jnp.dot(outer_prod.reshape(RT * RESIDUE_COUNT, OUTER_CHANNELS * OUTER_CHANNELS), covariance_exit_mapping.astype(jnp.float32))
        mixed_opm = mixed_opm.reshape(RT, RESIDUE_COUNT, PAIR_W)
        number = lax.dynamic_slice_in_dim(counts, block_start, RT, 0)
        return mixed_opm / (count_eps + number[:, :, None])
    starts = jnp.arange(N_ROW, dtype=jnp.int32) * RT
    outer_update = lax.map(opm_block, starts).reshape(RESIDUE_COUNT, RESIDUE_COUNT, PAIR_W)
    bucket = position_bins(peptide_ordinals, peptide_ordinals, strand_membership, strand_membership)
    z_one = coupling_activations.astype(jnp.float32) + distance_ordinal_vectors.astype(jnp.float32)[bucket] + outer_update
    ln_pair = zscore_transform(z_one)
    pair_bias = jnp.einsum('ijc,ch->hij', ln_pair, coupling_score_mapping.astype(jnp.float32), precision=lax.Precision.HIGHEST)
    bias_full = quantized_numbers(pair_bias)
    score_scale = 1.0 / math.sqrt(HEAD_CHANNELS)

    def homolog_softmax_mixing(row_inputs):
        normed, existing_lookup_marks = row_inputs
        queries = quantized_numbers(regrouped_covariance(normed, question_mapping_weights)).reshape(RESIDUE_COUNT, ATTENTION_HEADS, HEAD_CHANNELS)
        key_vals = quantized_numbers(regrouped_covariance(normed, address_payload_mapping))
        key_part = key_vals[:, :similarity_breadth].reshape(RESIDUE_COUNT, ATTENTION_HEADS, HEAD_CHANNELS)
        value_part = key_vals[:, similarity_breadth:].reshape(RESIDUE_COUNT, ATTENTION_HEADS, HEAD_CHANNELS)
        gate_activation = jax.nn.sigmoid(regrouped_covariance(normed, logistic_valve_mapping))
        scores = jnp.einsum('ihd,jhd->hij', queries, key_part) * score_scale + bias_full
        scores = jnp.where(existing_lookup_marks[None, None, :] > 0, scores, masked_score)
        maximal_precision = lax.optimization_barrier(jnp.max(scores, axis=-1, keepdims=True))
        exp_terms = jnp.exp(scores - maximal_precision)
        coefficient_accumulation = lax.optimization_barrier(jnp.sum(exp_terms, axis=-1))
        prob_terms = quantized_numbers(exp_terms)
        softmax_mixture = jnp.einsum('hij,jhd->ihd', prob_terms, value_part) / coefficient_accumulation.T[:, :, None]
        filtered_attended_result = (gate_activation * softmax_mixture.reshape(RESIDUE_COUNT, similarity_breadth)).astype(jnp.bfloat16)
        return jnp.dot(filtered_attended_result, mixture_exit_mapping, preferred_element_type=jnp.float32)
    additive_change = lax.map(homolog_softmax_mixing, (zscored_homologs, existing_homolog_marks))
    homologs_after = (homolog_activations.astype(jnp.float32) + additive_change).astype(jnp.bfloat16)
    ln_tri = ln_pair.astype(jnp.bfloat16)
    pair_live = (observed_peptide_marks[:, None] * observed_peptide_marks[None, :]).astype(jnp.float32)[:, :, None]
    side_left = regrouped_covariance(ln_tri, triad_opening_mappings[:, :2 * TRI_W])
    tri_left = quantized_numbers(jax.nn.sigmoid(side_left[:, :, TRI_W:]) * side_left[:, :, :TRI_W] * pair_live)
    side_right = regrouped_covariance(ln_tri, triad_opening_mappings[:, 2 * TRI_W:])
    tri_right = quantized_numbers(jax.nn.sigmoid(side_right[:, :, TRI_W:]) * side_right[:, :, :TRI_W] * pair_live)
    crossed = jnp.einsum('ikc,jkc->ijc', tri_left, tri_right)
    normed_cross = zscore_transform(crossed).astype(jnp.bfloat16)
    tri_proj = regrouped_covariance(normed_cross, triad_exit_mapping)
    tri_gate = jax.nn.sigmoid(regrouped_covariance(ln_tri, triad_valve_mapping))
    couplings_after = (z_one + tri_gate * tri_proj).astype(jnp.bfloat16)
    return (homologs_after, couplings_after)
```

```python
import functools
import math

import jax
import jax.numpy as jnp
from jax import lax
from jax.experimental import pallas as pl
from jax.experimental.pallas import tpu as pltpu
from jax.sharding import PartitionSpec as P

REL_MAX = 32
norm_eps = 1e-05
count_eps = 0.001
masked_score = -1000000000.0
LOG2E = 1.4426950408889634
MESH = pl.DeviceIdType.MESH
BF = jnp.bfloat16
F32 = jnp.float32

NR, NC = 16, 8
SQ, RB, CB = 16, 44, 88
RP = 48
WR = 2816 + 128
WL = 1408 + 128


def norm(v):
    v = v.astype(F32)
    v = v - jnp.mean(v, axis=-1, keepdims=True)
    return v * lax.rsqrt(jnp.mean(v * v, axis=-1, keepdims=True) + norm_eps)


def dot(a, b):
    return jnp.dot(a, b, preferred_element_type=F32)


def dot_nt(a, b):
    return lax.dot_general(a, b, (((1,), (1,)), ((), ())), preferred_element_type=F32)


def msa_kernel(
    x_ref, xt_ref, mr_ref, ml_ref, wc_ref, wp_ref, qk_ref, rall_ref, lall_ref,
    rmsg, lmsg, lsem, ssem, rsem,
):
    r = lax.axis_index("row")
    c = lax.axis_index("col")
    own = (r // 2) == c
    bar = pltpu.get_barrier_semaphore()
    for k in range(1, NR):
        pl.semaphore_signal(bar, inc=1, device_id=(r ^ k, c), device_id_type=MESH)
    @pl.when(jnp.logical_not(own))
    def _():
        for q in range(NR):
            pl.semaphore_signal(bar, inc=1, device_id=(jnp.int32(q), r // 2), device_id_type=MESH)

    rmsg[:, 2816:] = mr_ref[...]
    lmsg[0, :, 1408:] = ml_ref[0]
    lmsg[1, :, 1408:] = ml_ref[1]
    for g in range(22):
        y = dot(norm(xt_ref[64 * g : 64 * g + 64, :]).astype(BF), wc_ref[...])
        right = jnp.concatenate([y[16 * t : 16 * t + 16, 32:] for t in range(4)], axis=1)
        left = jnp.concatenate([y[16 * t : 16 * t + 16, :32] for t in range(4)], axis=1)
        rmsg[:, 128 * g : 128 * g + 128] = right.astype(BF)
        lmsg[g // 11, :, 128 * (g % 11) : 128 * (g % 11) + 128] = left.astype(BF)

    pl.semaphore_wait(bar, NR - 1 + 2 * (NC - 1))
    for k in range(1, NR):
        pltpu.make_async_remote_copy(
            rmsg, rall_ref.at[r], ssem.at[0], rsem.at[0], device_id=(r ^ k, c), device_id_type=MESH
        ).start()
    for h in range(2):
        for b in range(NC):
            here = jnp.logical_and(own, jnp.logical_and(r % 2 == h, c == b))
            @pl.when(here)
            def _():
                pltpu.make_async_copy(lmsg.at[h], lall_ref.at[r], rsem.at[1]).start()
            @pl.when(jnp.logical_not(here))
            def _():
                pltpu.make_async_remote_copy(
                    lmsg.at[h], lall_ref.at[r], ssem.at[1], rsem.at[1],
                    device_id=(2 * c + h, jnp.int32(b)), device_id_type=MESH,
                ).start()
    mine = pltpu.make_async_copy(rmsg, rall_ref.at[r], lsem)
    mine.start()

    for sg in range(4):
        ys = []
        for t in range(4):
            s = 4 * sg + t
            ys.append(dot(norm(x_ref[CB * s : CB * s + CB, :]).astype(BF), wp_ref[...]))
        for kind in range(4):
            for h in range(8):
                at = kind * 256 + h * 32
                piece = jnp.concatenate([y[:, at : at + 32] for y in ys], axis=1)
                qk_ref[h, sg, :, 128 * kind : 128 * kind + 128] = piece.astype(BF)

    mine.wait()
    pltpu.make_async_copy(rall_ref.at[pl.ds(0, NR - 1)], rall_ref.at[pl.ds(0, NR - 1)], rsem.at[0]).wait()
    pltpu.make_async_copy(lall_ref, lall_ref, rsem.at[1]).wait()
    pltpu.make_async_copy(rall_ref.at[pl.ds(0, NR - 1)], rall_ref.at[pl.ds(0, NR - 1)], ssem.at[0]).wait()
    @pl.when(own)
    def _():
        pltpu.make_async_copy(lall_ref.at[pl.ds(0, NR - 1)], lall_ref.at[pl.ds(0, NR - 1)], ssem.at[1]).wait()
    @pl.when(jnp.logical_not(own))
    def _():
        pltpu.make_async_copy(lall_ref, lall_ref, ssem.at[1]).wait()


def msa_stage(x, xt, mr, ml, wc, wp):
    vm = pl.BlockSpec(memory_space=pltpu.VMEM)
    return pl.pallas_call(
        msa_kernel,
        out_shape=(
            jax.ShapeDtypeStruct((8, 4, CB, 512), BF),
            jax.ShapeDtypeStruct((NR, SQ, WR), BF),
            jax.ShapeDtypeStruct((NR, SQ, WL), BF),
        ),
        in_specs=[vm] * 6,
        out_specs=(vm,) * 3,
        scratch_shapes=[
            pltpu.VMEM((SQ, WR), BF),
            pltpu.VMEM((2, SQ, WL), BF),
            pltpu.SemaphoreType.DMA,
            pltpu.SemaphoreType.DMA((2,)),
            pltpu.SemaphoreType.DMA((2,)),
        ],
        compiler_params=pltpu.CompilerParams(
            collective_id=0, has_side_effects=True, vmem_limit_bytes=40 << 20
        ),
    )(x, xt, mr, ml, wc, wp)


def attention_kernel(qk_ref, bias_ref, madd_ref, out_ref, kbuf, vbuf):
    cb = pl.program_id(1)
    lane = lax.broadcasted_iota(jnp.int32, (CB, 128), 1) // 32

    @pl.when(cb == 0)
    def _():
        for b in range(NC):
            kbuf[CB * b : CB * b + CB, :] = qk_ref[b, 0, :, 128:256].astype(F32)
            vbuf[CB * b : CB * b + CB, :] = qk_ref[b, 0, :, 256:384].astype(F32)

    qg = qk_ref[cb, 0].astype(F32)
    keys = kbuf[...].astype(BF)
    vals = jnp.concatenate([vbuf[...].astype(BF), jnp.ones((704, 128), BF)], axis=1)
    bias = bias_ref[...].astype(F32)
    acc = jnp.zeros((CB, 128), F32)
    for t in range(4):
        q = jnp.where(lane == t, qg[:, :128], 0.0).astype(BF)
        s = dot_nt(q, keys) + bias + madd_ref[0, t : t + 1, :]
        p = jnp.exp2(s - jnp.max(s, axis=-1, keepdims=True)).astype(BF)
        o = dot(p, vals)
        acc = jnp.where(lane == t, o[:, :128] / o[:, 128:], acc)
    gate = jax.nn.sigmoid(qg[:, 384:])
    out_ref[0, 0] = (gate * acc).astype(BF)


def attention(qk, bias, madd):
    return pl.pallas_call(
        attention_kernel,
        out_shape=jax.ShapeDtypeStruct((NC, 4, CB, 128), BF),
        grid=(4, NC),
        in_specs=[
            pl.BlockSpec((NC, 1, CB, 512), lambda g, b: (0, g, 0, 0)),
            pl.BlockSpec((CB, 704), lambda g, b: (b, 0)),
            pl.BlockSpec((1, 4, 704), lambda g, b: (g, 0, 0)),
        ],
        out_specs=pl.BlockSpec((1, 1, CB, 128), lambda g, b: (b, g, 0, 0)),
        scratch_shapes=[pltpu.VMEM((704, 128), F32)] * 2,
        compiler_params=pltpu.CompilerParams(vmem_limit_bytes=40 << 20),
    )(qk, bias, madd)


def mix_kernel(g_ref, x_ref, w_ref, out_ref):
    lane = lax.broadcasted_iota(jnp.int32, (CB, 1024), 1) % 128 // 32
    cat = jnp.concatenate([g_ref[h, 0].astype(F32) for h in range(8)], axis=1)
    for t in range(4):
        y = dot(jnp.where(lane == t, cat, 0.0).astype(BF), w_ref[...])
        out_ref[t] = (x_ref[t].astype(F32) + y).astype(BF)


def mix(g, x, w):
    return pl.pallas_call(
        mix_kernel,
        out_shape=jax.ShapeDtypeStruct((SQ, CB, 256), BF),
        grid=(4,),
        in_specs=[
            pl.BlockSpec((8, 1, CB, 128), lambda g: (0, g, 0, 0)),
            pl.BlockSpec((4, CB, 256), lambda g: (g, 0, 0)),
            pl.BlockSpec((1024, 256), lambda g: (0, 0)),
        ],
        out_specs=pl.BlockSpec((4, CB, 256), lambda g: (g, 0, 0)),
    )(g, x, w)


def tri_kernel(t_ref, out_ref):
    for pair in range(4):
        acc = None
        for b in range(0, NC, 2):
            lhs = jnp.concatenate(
                [t_ref[:, b + d, 0].reshape(NR * RP, 128) for d in range(2)], axis=1
            )
            rhs = jnp.concatenate(
                [t_ref[4 * pair : 4 * pair + 4, b + d, 1].reshape(4 * RP, 128) for d in range(2)], axis=1
            )
            y = dot_nt(lhs, rhs)
            acc = y if acc is None else acc + y
        for h in range(2):
            at = 96 * h
            row = jnp.concatenate(
                [acc[:, at : at + 44], acc[:, at + 48 : at + 92], jnp.zeros((NR * RP, 40), F32)], axis=1
            )
            out_ref[:, 2 * pair + h] = row.astype(BF).reshape(NR, RP, 128)


def tri(t):
    vm = pl.BlockSpec(memory_space=pltpu.VMEM)
    return pl.pallas_call(
        tri_kernel,
        out_shape=jax.ShapeDtypeStruct((NR, NC, RP, 128), BF),
        in_specs=[vm],
        out_specs=vm,
        compiler_params=pltpu.CompilerParams(vmem_limit_bytes=40 << 20),
    )(t)


def flat_dot(operand, weights):
    result = dot(operand.reshape(-1, operand.shape[-1]), weights)
    return result.reshape(operand.shape[:-1] + (weights.shape[-1],))


def shards(
    msa, pair, marks, res_marks, ordinals, strand, dist_vectors, w_bias, w_q, w_kv, w_gate, w_mix,
    w_cov, w_opm, w_tri, w_valve, w_exit,
):
    r = lax.axis_index("row")
    c = lax.axis_index("col")
    marks_b = marks.astype(BF)
    xt = jnp.swapaxes(jnp.where(marks[:, :, None] > 0, msa, jnp.zeros_like(msa)), 0, 1)
    mr = jnp.pad(marks_b, ((0, 0), (0, 128 - CB)))
    ml = jnp.stack([jnp.pad(marks_b[:, RB * h : RB * h + RB], ((0, 0), (0, 128 - RB))) for h in range(2)])
    scale = LOG2E / math.sqrt(32.0)
    wp = jnp.concatenate([(w_q.astype(F32) * scale).astype(BF), w_kv, w_gate], axis=1)
    qk, rall, lall = msa_stage(
        msa.reshape(SQ * CB, 256), xt.reshape(SQ * CB, 256), mr, ml, w_cov, wp
    )
    qk = lax.all_to_all(qk, "col", 0, 0, tiled=True)
    every_marks = lax.all_gather(marks, "col", axis=1, tiled=True)
    madd = jnp.where(every_marks > 0, 0.0, masked_score).astype(F32).reshape(4, 4, 704)

    rall = rall.reshape(256, WR)
    lall = lall.reshape(256, WL)
    counts = dot(lall[:, 1408 : 1408 + RB].T, rall[:, 2816 : 2816 + CB])
    outer = jnp.einsum(
        "sic,sje->ijce",
        lall[:, :1408].reshape(256, RB, 32),
        rall[:, :2816].reshape(256, CB, 32),
        preferred_element_type=F32,
    ).astype(BF)
    update = flat_dot(outer.reshape(RB, CB, 1024), w_opm) / (count_eps + counts[:, :, None])
    row_first, col_first = r * RB, c * CB
    cut_r = lambda v: lax.dynamic_slice_in_dim(v, row_first, RB)
    cut_c = lambda v: lax.dynamic_slice_in_dim(v, col_first, CB)
    bins = jnp.clip(cut_r(ordinals)[:, None] - cut_c(ordinals)[None, :] + REL_MAX, 0, 2 * REL_MAX)
    bins = jnp.where(cut_r(strand)[:, None] == cut_c(strand)[None, :], bins, 2 * REL_MAX + 1)
    one_hot = (bins[:, :, None] == jnp.arange(dist_vectors.shape[0], dtype=jnp.int32)).astype(BF)
    z_one = pair.astype(F32) + flat_dot(one_hot, dist_vectors) + update
    ln_pair = norm(z_one)
    bias = jnp.einsum("ijc,ch->hij", ln_pair, w_bias.astype(F32), precision=lax.Precision.HIGHEST)
    bias = (bias * LOG2E).astype(BF)
    bias = lax.all_to_all(bias, "col", 0, 0, tiled=True)
    bias = lax.all_gather(bias, "row", axis=0, tiled=False)
    bias = bias.transpose(0, 2, 1, 3).reshape(704, 704)

    ln_tri = ln_pair.astype(BF)
    live = (cut_r(res_marks)[:, None] * cut_c(res_marks)[None, :]).astype(F32)
    side = jnp.einsum("ijc,cd->dij", ln_tri, w_tri, preferred_element_type=F32)
    t_left = (jax.nn.sigmoid(side[128:256]) * side[:128] * live).astype(BF)
    t_right = (jax.nn.sigmoid(side[384:]) * side[256:384] * live).astype(BF)
    both = jnp.stack([t_left, t_right], axis=1)
    both = jnp.pad(both, ((0, 0), (0, 0), (0, RP - RB), (0, 128 - CB)))
    both = lax.all_to_all(both, ("row", "col"), 0, 0, tiled=True)
    crossed = tri(both.reshape(NR, NC, 2, RP, 128))
    crossed = lax.all_to_all(crossed.reshape(128, RP, 128), ("row", "col"), 0, 0, tiled=True)
    crossed = crossed[:, :RB, :CB].astype(F32)
    crossed = crossed - jnp.mean(crossed, axis=0, keepdims=True)
    crossed = crossed * lax.rsqrt(jnp.mean(crossed * crossed, axis=0, keepdims=True) + norm_eps)
    proj = jnp.einsum("cij,cf->ijf", crossed.astype(BF), w_exit, preferred_element_type=F32)
    gate = jax.nn.sigmoid(flat_dot(ln_tri, w_valve))
    pair_out = (z_one + gate * proj).astype(BF)

    gated = attention(qk, bias, madd)
    gated = lax.all_to_all(gated, "col", 0, 0, tiled=True)
    w_rep = jnp.broadcast_to(w_mix.reshape(8, 1, 32, 256), (8, 4, 32, 256)).reshape(1024, 256)
    return mix(gated, msa, w_rep), pair_out


def solution(mesh):
    placed = (P("row", "col", None), P("row", "col", None), P("row", "col")) + (P(),) * 14
    return jax.shard_map(
        shards,
        mesh=mesh,
        in_specs=placed,
        out_specs=(P("row", "col", None), P("row", "col", None)),
        check_vma=False,
    )
```

```python
import math

import jax
import jax.numpy as jnp
from jax import lax
from jax.experimental import pallas as pl
from jax.experimental.pallas import tpu as pltpu
from jax.sharding import PartitionSpec as P

REL_MAX = 32
norm_eps = 1e-05
count_eps = 0.001
masked_score = -1000000000.0
LOG2E = 1.4426950408889634
MESH = pl.DeviceIdType.MESH
BF = jnp.bfloat16
F32 = jnp.float32

NR, NC = 16, 8
ND = NR * NC
SQ, RB, CB = 16, 44, 88
N = 704
RP = 48
WR = 2816 + 128
WL = 1408 + 128
S_R, S_L, S_QK, S_MK, S_B, S_T, S_G, S_X = range(8)


def norm(v):
    v = v.astype(F32)
    v = v - jnp.mean(v, axis=-1, keepdims=True)
    return v * lax.rsqrt(jnp.mean(v * v, axis=-1, keepdims=True) + norm_eps)


def dot(a, b):
    return jnp.dot(a, b, preferred_element_type=F32)


def dot_nt(a, b):
    return lax.dot_general(a, b, (((1,), (1,)), ((), ())), preferred_element_type=F32)


def dot_tn(a, b):
    return lax.dot_general(a, b, (((0,), (0,)), ((), ())), preferred_element_type=F32)


def iota(shape, dim):
    return lax.broadcasted_iota(jnp.int32, shape, dim)


def loop(low, high, body):
    def step(k, carry):
        body(k)
        return carry

    lax.fori_loop(low, high, step, 0)


def kernel(
    x_ref, pair_ref, mr_ref, ml_ref, scal_ref, colv_ref, live_ref, w_cov, w_q, w_kv, w_gate, w_mix,
    w_opm, dist_ref, w_all, w_valve, w_exit,
    out_a, out_b,
    zs0, zs1, zb, lhs_r, wbd_r, wbd_l, rmsg, lmsg, qmsg, bd, rt, xs, xb, acc_ref, zscr, hb, st_l, st_r,
    st_b, bmsg, tmsg, kf, kb, vb, biasbuf, gmsg, tout,
    rall, lall, qrecv, mrecv, brecv, trecv, grecv, xrecv,
    ssem, rsem,
):
    r = lax.axis_index("row")
    c = lax.axis_index("col")
    me = r * NC + c
    own = (r // 2) == c

    def send(src, dst, kind, rr, cc):
        pltpu.make_async_remote_copy(
            src, dst, ssem.at[kind], rsem.at[kind], device_id=(rr, cc), device_id_type=MESH
        ).start()

    def keep(src, dst, kind):
        pltpu.make_async_copy(src, dst, rsem.at[kind]).start()

    def arrived(ref, kind):
        pltpu.make_async_copy(ref, ref, rsem.at[kind]).wait()

    def sent(ref, kind):
        pltpu.make_async_copy(ref, ref, ssem.at[kind]).wait()

    bar = pltpu.get_barrier_semaphore()

    @pl.loop(1, ND)
    def _(k):
        pl.semaphore_signal(bar, inc=1, device_id=(r ^ (k // NC), c ^ (k % NC)), device_id_type=MESH)

    def msa_norm(s):
        v = norm(x_ref[s])
        at = pl.ds(pl.multiple_of(s * CB, 8), CB)
        zs0[at, :] = v[:, :128]
        zs1[at, :] = v[:, 128:]
        zb[s] = v.astype(BF)

    loop(0, SQ, msa_norm)

    cov = w_cov[...]
    for j in range(8):
        pick = (iota((32, 256), 1) == 8 * iota((32, 256), 0) + j).astype(BF)
        wbd_r[256 * j : 256 * j + 256, :] = dot(cov[:, 32:], pick).astype(BF)
    for j in range(4):
        pick = (iota((32, 128), 1) == 32 * j + iota((32, 128), 0)).astype(BF)
        wbd_l[256 * j : 256 * j + 256, :] = dot(cov[:, :32], pick).astype(BF)
    marks = mr_ref[...].astype(F32)
    for j in range(CB):
        g, b = j // 8, j % 8
        m = jnp.broadcast_to(marks[:, j : j + 1], (SQ, 128))
        lhs_r[16 * g : 16 * g + 16, 256 * b : 256 * b + 128] = (zs0[pl.ds(j, SQ, stride=CB), :] * m).astype(BF)
        lhs_r[16 * g : 16 * g + 16, 256 * b + 128 : 256 * b + 256] = (
            zs1[pl.ds(j, SQ, stride=CB), :] * m
        ).astype(BF)
    y = dot(lhs_r[...], wbd_r[...]).astype(BF)
    for g in range(11):
        rmsg[:, 256 * g : 256 * g + 256] = y[16 * g : 16 * g + 16]
    for b in range(2):
        y = dot(lhs_r[:, 1024 * b : 1024 * b + 1024], wbd_l[...]).astype(BF)
        for jg in range(11):
            g = 2 * jg + b
            lmsg[g // 11, :, 128 * (g % 11) : 128 * (g % 11) + 128] = y[16 * jg : 16 * jg + 16]
    rmsg[:, 2816:] = mr_ref[...]
    lmsg[0, :, 1408:] = ml_ref[0]
    lmsg[1, :, 1408:] = ml_ref[1]

    pl.semaphore_wait(bar, ND - 1)

    keep(rmsg, rall.at[r], S_R)
    for k in range(1, NR):
        send(rmsg, rall.at[r], S_R, r ^ k, c)
    for h in range(2):
        for b in range(NC):
            here = jnp.logical_and(own, jnp.logical_and(r % 2 == h, c == b))

            @pl.when(here)
            def _():
                keep(lmsg.at[h], lall.at[r], S_L)

            @pl.when(jnp.logical_not(here))
            def _():
                send(lmsg.at[h], lall.at[r], S_L, 2 * c + h, jnp.int32(b))

    scale = LOG2E / math.sqrt(32.0)

    def project(sg):
        ys = []
        for t in range(4):
            v = zb[4 * sg + t]
            kv = dot(v, w_kv[...])
            ys.append((dot(v, w_q[...]) * scale, kv[:, :256], kv[:, 256:], dot(v, w_gate[...])))
        for kind in range(4):
            for h in range(8):
                piece = jnp.concatenate([y[kind][:, 32 * h : 32 * h + 32] for y in ys], axis=1)
                qmsg[h, sg, :, 128 * kind : 128 * kind + 128] = piece.astype(BF)

    loop(0, 4, project)
    keep(qmsg.at[c], qrecv.at[c], S_QK)
    keep(mr_ref, mrecv.at[c], S_MK)
    for k in range(1, NC):
        send(mr_ref, mrecv.at[c], S_MK, r, c ^ k)
        send(qmsg.at[c ^ k], qrecv.at[c], S_QK, r, c ^ k)

    bd[...] = jnp.zeros_like(bd)

    arrived(rall, S_R)
    arrived(lall, S_L)
    for g in range(22):
        rt[128 * g : 128 * g + 128, :] = rall[:, :, 128 * g : 128 * g + 128].reshape(256, 128).T
    counts = dot_tn(
        rall[:, :, 2816:].reshape(256, 128), lall[:, :, 1408:].reshape(256, 128)
    ).astype(BF)
    for ig in range(6):
        lhs = lall[:, :, 256 * ig : 256 * ig + 256].reshape(256, 256)
        for part in range(4):
            at = slice(N * part, N * part + N)
            xs[at, :] = dot(rt[at, :], lhs)

        def regroup(e):
            rows = [xs[pl.ds(pl.multiple_of(256 * g + 8 * e, 8), 8), :] for g in range(11)]
            rows.append(jnp.zeros((8, 256), F32))
            xb[e, 96 * ig : 96 * ig + 96, :] = jnp.concatenate(rows, axis=0).astype(BF)

        loop(0, 32, regroup)

    for ec in range(4):
        for e in range(8):
            for i in range(8):
                bd[256 * e + 32 * i : 256 * e + 32 * i + 32, 128 * i : 128 * i + 128] = w_opm[8 * ec + e]
        for part in range(3):
            at = slice(192 * part, 192 * part + 192)
            lhs = jnp.concatenate([xb[8 * ec + e, at, :] for e in range(8)], axis=1)
            for n in range(4):
                y = dot(lhs, bd[:, 256 * n : 256 * n + 256])
                if ec:
                    acc_ref[at, 256 * n : 256 * n + 256] += y
                else:
                    acc_ref[at, 256 * n : 256 * n + 256] = y

    ordinals, strands = colv_ref[0], colv_ref[1]
    lane = iota((CB, 128), 1)
    fill = jnp.zeros((128 - CB, 128), F32)

    def wide(v):
        return jnp.concatenate([v, fill], axis=0).astype(BF)

    def pair_rows(ig, number):
        pick = (iota((128, 1024), 0) == 8 * ig + iota((128, 1024), 1) // 128).astype(BF)
        weight = 1.0 / (count_eps + dot(counts, pick)[:CB])
        rows = pl.ds(pl.multiple_of(96 * ig, 8), CB)
        for b in range(number):
            i = 8 * ig + b
            bins = jnp.clip(scal_ref[0, i] - ordinals + REL_MAX, 0, 2 * REL_MAX)
            bins = jnp.where(strands == scal_ref[1, i], bins, 2 * REL_MAX + 1)
            z = pair_ref[i].astype(F32) + dot((bins == lane).astype(BF), dist_ref[...])
            z = z + acc_ref[rows, 128 * b : 128 * b + 128] * weight[:, 128 * b : 128 * b + 128]
            zscr[i] = z
            v = norm(z)
            high = wide(v)
            low = (jnp.concatenate([v, fill], axis=0) - high.astype(F32)).astype(BF)
            hb[i] = high
            bias = dot_nt(w_all[512:528, :], high) + dot_nt(w_all[512:528, :], low)
            st_b[pl.ds(i, 8, stride=RP), :] = bias[:8] * LOG2E

    loop(0, 5, lambda ig: pair_rows(ig, 8))
    pair_rows(5, 4)

    for h in range(8):
        bmsg[h] = st_b[RP * h : RP * h + RP, :].astype(BF)
    keep(bmsg.at[c], brecv.at[me], S_B)

    @pl.loop(1, ND)
    def _(k):
        rr, cc = r ^ (k // NC), c ^ (k % NC)
        send(bmsg.at[cc], brecv.at[me], S_B, rr, cc)

    live = live_ref[...]

    def tri_rows(i):
        y = dot_nt(w_all[:512, :], hb[i])
        alive = live * scal_ref[2, i].astype(F32)
        st_l[pl.ds(i, 128, stride=RP), :] = jax.nn.sigmoid(y[128:256]) * y[:128] * alive
        st_r[pl.ds(i, 128, stride=RP), :] = jax.nn.sigmoid(y[384:]) * y[256:384] * alive

    loop(0, RB, tri_rows)

    def tri_pack(ch):
        at = pl.ds(pl.multiple_of(RP * ch, 8), RP)
        tmsg[ch, 0] = st_l[at, :].astype(BF)
        tmsg[ch, 1] = st_r[at, :].astype(BF)

    loop(0, ND, tri_pack)
    keep(tmsg.at[me], trecv.at[me], S_T)

    @pl.loop(1, ND)
    def _(k):
        rr, cc = r ^ (k // NC), c ^ (k % NC)
        send(tmsg.at[rr * NC + cc], trecv.at[me], S_T, rr, cc)

    arrived(qrecv, S_QK)
    arrived(mrecv, S_MK)

    def gather_keys(sg):
        for b in range(NC):
            kf[CB * b : CB * b + CB, :] = qrecv[b, sg, :, 128:256].astype(F32)
        kb[sg] = kf[...].astype(BF)
        for b in range(NC):
            kf[CB * b : CB * b + CB, :] = qrecv[b, sg, :, 256:384].astype(F32)
        vb[sg, :, :128] = kf[...].astype(BF)
        vb[sg, :, 128:] = jnp.ones((N, 128), BF)

    loop(0, 4, gather_keys)
    every = jnp.concatenate([mrecv[b].astype(F32)[:, :CB] for b in range(NC)], axis=1)
    madd = jnp.where(every > 0, 0.0, masked_score)
    group = lane // 32
    arrived(brecv, S_B)

    def attend(k):
        cb = c ^ k
        halves = []
        for d in range(2):
            row = [brecv[(2 * cb + d) * NC + b].astype(F32)[:RB, :CB] for b in range(NC)]
            halves.append(jnp.concatenate(row, axis=1))
        biasbuf[...] = jnp.concatenate(halves, axis=0)
        for sg in range(4):
            own_q = qrecv[cb, sg].astype(F32)
            q = jnp.concatenate([jnp.where(group == t, own_q[:, :128], 0.0) for t in range(4)], axis=0)
            s = dot_nt(q.astype(BF), kb[sg])
            ps = []
            for t in range(4):
                v = s[CB * t : CB * t + CB] + biasbuf[...] + madd[4 * sg + t : 4 * sg + t + 1]
                ps.append(jnp.exp2(v - jnp.max(v, axis=-1, keepdims=True)))
            o = dot(jnp.concatenate(ps, axis=0).astype(BF), vb[sg])
            o = o[:, :128] / o[:, 128:]
            mixed = o[:CB]
            for t in range(1, 4):
                mixed = jnp.where(group == t, o[CB * t : CB * t + CB], mixed)
            gmsg[cb, sg] = (jax.nn.sigmoid(own_q[:, 384:]) * mixed).astype(BF)

        @pl.when(k == 0)
        def _():
            keep(gmsg.at[c], grecv.at[c], S_G)

        @pl.when(k > 0)
        def _():
            send(gmsg.at[cb], grecv.at[c], S_G, r, cb)

    loop(0, NC, attend)

    arrived(trecv, S_T)
    for pair in range(4):
        total = None
        for b in range(0, NC, 2):
            lhs, rhs = [], []
            for d in range(2):
                lhs.append(jnp.concatenate([trecv[q * NC + b + d, 0] for q in range(NR)], axis=0))
                rhs.append(jnp.concatenate([trecv[(4 * pair + q) * NC + b + d, 1] for q in range(4)], axis=0))
            y = dot_nt(jnp.concatenate(lhs, axis=1), jnp.concatenate(rhs, axis=1))
            total = y if total is None else total + y
        for h in range(2):
            at = 96 * h
            row = jnp.concatenate(
                [total[:, at : at + RB], total[:, at + RP : at + RP + RB], jnp.zeros((NR * RP, 128 - CB), F32)],
                axis=1,
            ).astype(BF)
            for q in range(NR):
                tout[q * NC + 2 * pair + h] = row[RP * q : RP * q + RP]

        @pl.loop(0, 2 * NR)
        def _(k):
            rr, cc = r ^ (k // 2), 2 * pair + k % 2
            here = jnp.logical_and(rr == r, cc == c)

            @pl.when(here)
            def _():
                keep(tout.at[me], xrecv.at[me], S_X)

            @pl.when(jnp.logical_not(here))
            def _():
                send(tout.at[rr * NC + cc], xrecv.at[me], S_X, rr, cc)

    arrived(grecv, S_G)
    w_rep = []
    for h in range(8):
        w_rep += [w_mix[32 * h : 32 * h + 32, :]] * 4
    w_rep = jnp.concatenate(w_rep, axis=0)
    wide_group = iota((CB, 1024), 1) % 128 // 32

    def mix(sg):
        cat = jnp.concatenate([grecv[h, sg].astype(F32) for h in range(8)], axis=1)
        for t in range(4):
            y = dot(jnp.where(wide_group == t, cat, 0.0).astype(BF), w_rep)
            out_a[4 * sg + t] = (x_ref[4 * sg + t].astype(F32) + y).astype(BF)

    loop(0, 4, mix)

    arrived(xrecv, S_X)
    for part in range(3):
        rows = slice(16 * part, 16 * part + 16)
        total = lax.fori_loop(
            0, ND, lambda ch, t: t + xrecv[ch, rows, :].astype(F32), jnp.zeros((16, 128), F32)
        )
        mean = total * (1.0 / 128)

        def square(ch, t):
            d = xrecv[ch, rows, :].astype(F32) - mean
            return t + d * d

        total = lax.fori_loop(0, ND, square, jnp.zeros((16, 128), F32))
        inv = lax.rsqrt(total * (1.0 / 128) + norm_eps)

        def scaled(ch):
            at = pl.ds(pl.multiple_of(RP * ch + 16 * part, 8), 16)
            st_l[at, :] = (xrecv[ch, rows, :].astype(F32) - mean) * inv

        loop(0, ND, scaled)

    def last(i):
        cross = st_l[pl.ds(i, 128, stride=RP), :].astype(BF)
        proj = dot_tn(cross, w_exit[...])[:CB]
        gate = jax.nn.sigmoid(dot(hb[i], w_valve[...])[:CB])
        out_b[i] = (zscr[i] + gate * proj).astype(BF)

    loop(0, RB, last)

    sent(rall.at[pl.ds(0, NR - 1)], S_R)

    @pl.when(own)
    def _():
        sent(lall.at[pl.ds(0, NR - 1)], S_L)

    @pl.when(jnp.logical_not(own))
    def _():
        sent(lall, S_L)

    sent(qrecv.at[pl.ds(0, NC - 1)], S_QK)
    sent(mrecv.at[pl.ds(0, NC - 1)], S_MK)
    sent(brecv.at[pl.ds(0, ND - 1)], S_B)
    sent(trecv.at[pl.ds(0, ND - 1)], S_T)
    sent(grecv.at[pl.ds(0, NC - 1)], S_G)
    sent(xrecv.at[pl.ds(0, ND - 1)], S_X)


def run(*operands):
    vm = pl.BlockSpec(memory_space=pltpu.VMEM)
    sm = pl.BlockSpec(memory_space=pltpu.SMEM)
    V = pltpu.VMEM
    scratch = [
        V((SQ * CB, 128), F32), V((SQ * CB, 128), F32), V((SQ, CB, 256), BF),
        V((176, 2048), BF), V((2048, 256), BF), V((1024, 128), BF),
        V((SQ, WR), BF), V((2, SQ, WL), BF), V((8, 4, CB, 512), BF),
        V((2048, 1024), BF), V((2816, 256), BF), V((2816, 256), F32),
        V((32, 576, 256), BF), V((576, 1024), F32),
        V((RB, CB, 128), F32), V((RB, 128, 128), BF),
        V((ND * RP, 128), F32), V((ND * RP, 128), F32), V((8 * RP, 128), F32),
        V((8, RP, 128), BF), V((ND, 2, RP, 128), BF),
        V((N, 128), F32), V((4, N, 128), BF), V((4, N, 256), BF), V((CB, N), F32),
        V((NC, 4, CB, 128), BF), V((ND, RP, 128), BF),
        V((NR, SQ, WR), BF), V((NR, SQ, WL), BF), V((NC, 4, CB, 512), BF), V((NC, SQ, 128), BF),
        V((ND, RP, 128), BF), V((ND, 2, RP, 128), BF), V((NC, 4, CB, 128), BF), V((ND, RP, 128), BF),
        pltpu.SemaphoreType.DMA((8,)), pltpu.SemaphoreType.DMA((8,)),
    ]
    return pl.pallas_call(
        kernel,
        out_shape=(
            jax.ShapeDtypeStruct((SQ, CB, 256), BF),
            jax.ShapeDtypeStruct((RB, CB, 128), BF),
        ),
        in_specs=[vm] * 4 + [sm] + [vm] * 12,
        out_specs=(vm, vm),
        scratch_shapes=scratch,
        compiler_params=pltpu.CompilerParams(
            collective_id=0, has_side_effects=True, vmem_limit_bytes=63 << 20
        ),
    )(*operands)


def shards(
    msa, pair, marks, res_marks, ordinals, strand, dist_vectors, w_bias, w_q, w_kv, w_gate, w_mix,
    w_cov, w_opm, w_tri, w_valve, w_exit,
):
    r = lax.axis_index("row")
    c = lax.axis_index("col")
    marks_b = marks.astype(BF)
    mr = jnp.pad(marks_b, ((0, 0), (0, 128 - CB)))
    ml = jnp.stack([jnp.pad(marks_b[:, RB * h : RB * h + RB], ((0, 0), (0, 128 - RB))) for h in range(2)])
    three = jnp.stack([ordinals, strand, res_marks])
    scal = lax.dynamic_slice_in_dim(three, r * RB, RB, 1)
    cols = lax.dynamic_slice_in_dim(three, c * CB, CB, 1)
    colv = jnp.broadcast_to(cols[:2, :, None], (2, CB, 128))
    live = jnp.pad(cols[2:].astype(F32), ((0, 0), (0, 128 - CB)))
    w_opm_e = w_opm.reshape(32, 32, 128).swapaxes(0, 1)
    dist = jnp.pad(dist_vectors, ((0, 128 - dist_vectors.shape[0]), (0, 0)))
    w_all = jnp.concatenate([w_tri.T, jnp.pad(w_bias.T, ((0, 8), (0, 0)))], axis=0)
    return run(
        msa, pair, mr, ml, scal, colv, live, w_cov, w_q, w_kv, w_gate, w_mix, w_opm_e, dist, w_all,
        w_valve, w_exit,
    )


def solution(mesh):
    placed = (P("row", "col", None), P("row", "col", None), P("row", "col")) + (P(),) * 14
    return jax.shard_map(
        shards,
        mesh=mesh,
        in_specs=placed,
        out_specs=(P("row", "col", None), P("row", "col", None)),
        check_vma=False,
    )
```

```python
import math

import jax
import jax.numpy as jnp
from jax import lax
from jax.experimental import pallas as pl
from jax.experimental.pallas import tpu as pltpu
from jax.sharding import PartitionSpec as P

REL_MAX = 32
norm_eps = 1e-05
count_eps = 0.001
masked_score = -1000000000.0
LOG2E = 1.4426950408889634
MESH = pl.DeviceIdType.MESH
BF = jnp.bfloat16
F32 = jnp.float32

NR, NC = 16, 8
ND = NR * NC
SQ, RB, CB = 16, 44, 88
N = 704
RP = 48
WR = 2816 + 128
WL = 1408 + 128
S_R, S_R2, S_L, S_QK, S_MK, S_B, S_B2, S_TL, S_TR, S_G, S_X = range(11)
PK = 32


def norm(v):
    v = v.astype(F32)
    v = v - jnp.mean(v, axis=-1, keepdims=True)
    return v * lax.rsqrt(jnp.mean(v * v, axis=-1, keepdims=True) + norm_eps)


def dot(a, b):
    return jnp.dot(a, b, preferred_element_type=F32)


def dot_nt(a, b):
    return lax.dot_general(a, b, (((1,), (1,)), ((), ())), preferred_element_type=F32)


def dot_tn(a, b):
    return lax.dot_general(a, b, (((0,), (0,)), ((), ())), preferred_element_type=F32)


def iota(shape, dim):
    return lax.broadcasted_iota(jnp.int32, shape, dim)


def loop(low, high, body, unroll=1):
    def step(k, carry):
        body(k)
        return carry

    lax.fori_loop(low, high, step, 0, unroll=unroll)


def roll(v, lanes):
    return pltpu.roll(v, lanes, 1)


def pack(u):
    lane, sub = iota((8, 128), 1), iota((8, 128), 0)
    extra = (
        roll(u[4], 88),
        roll(u[4], 48),
        jnp.where(sub < 4, roll(u[5], 88), pltpu.roll(roll(u[5], 48), 4, 0)),
        jnp.where(lane < 96, roll(u[4], 8), roll(u[5], 16)),
    )
    return jnp.concatenate([jnp.where(lane < CB, u[k], extra[k]) for k in range(4)], axis=0)


def unpack(p):
    lane = iota((8, 128), 1)
    p = [p[8 * k : 8 * k + 8] for k in range(4)]
    low, mid, high = lane < 40, lane < 80, lane < CB
    u = [jnp.where(high, v, 0.0) for v in p]
    tail = jnp.where(high, roll(p[3], 120), 0.0)
    u.append(jnp.where(low, roll(p[0], 40), jnp.where(mid, roll(p[1], 80), tail)))
    tail = jnp.where(high, roll(p[3], 112), 0.0)
    u.append(jnp.where(low, roll(p[2], 40), jnp.where(mid, pltpu.roll(roll(p[2], 80), 4, 0), tail)))
    return u


def kernel(
    x_ref, pair_ref, marks_ref, code_ref, code_col, w_cov, w_q, w_kv, w_gate, w_mix,
    w_opm, dist_ref, w_tri, w_bias, w_valve, w_exit,
    out_a, out_b,
    zs0, zs1, zb, lhs_r, wbd_r, wbd_l, w_all, w_opm_e, gates, mmsg, rmsg, lmsg, qmsg, bd, rt, xs, xb, acc_ref,
    zscr, hb, st, st_b, bmsg, tl_msg, tr_msg, kf, kb, vb, biasbuf, gmsg, lbuf, rbuf, pbuf, tout, stats,
    rall, lall, qrecv, mrecv, brecv, tl_recv, tr_recv, grecv, xrecv,
    ssem, rsem,
):
    r = lax.axis_index("row")
    c = lax.axis_index("col")
    me = r * NC + c
    own = (r // 2) == c

    def send(src, dst, kind, rr, cc):
        pltpu.make_async_remote_copy(
            src, dst, ssem.at[kind], rsem.at[kind], device_id=(rr, cc), device_id_type=MESH
        ).start()

    def keep(src, dst, kind):
        pltpu.make_async_copy(src, dst, rsem.at[kind]).start()

    def arrived(ref, kind):
        pltpu.make_async_copy(ref, ref, rsem.at[kind]).wait()

    def sent(ref, kind):
        pltpu.make_async_copy(ref, ref, ssem.at[kind]).wait()

    bar = pltpu.get_barrier_semaphore()

    @pl.loop(1, ND)
    def _(k):
        pl.semaphore_signal(bar, inc=1, device_id=(r ^ (k // NC), c ^ (k % NC)), device_id_type=MESH)

    for k in range(4):
        w_all[128 * k : 128 * k + 128, :] = w_tri[:, 128 * k : 128 * k + 128].T
    w_all[512:, :] = jnp.concatenate([w_bias[...].astype(F32), jnp.zeros((8, 128), F32)], axis=0).astype(BF)

    def msa_norm(s):
        v = norm(x_ref[s])
        at = pl.ds(pl.multiple_of(s * CB, 8), CB)
        zs0[at, :] = v[:, :128]
        zs1[at, :] = v[:, 128:]
        zb[s] = v.astype(BF)

    loop(0, SQ, msa_norm)

    cov = w_cov[...]
    for j in range(8):
        pick = (iota((32, 256), 1) == 8 * iota((32, 256), 0) + j).astype(BF)
        wbd_r[256 * j : 256 * j + 256, :] = dot_tn(cov[32:], pick).astype(BF)
    for j in range(4):
        pick = (iota((32, 128), 1) == 32 * j + iota((32, 128), 0)).astype(BF)
        wbd_l[256 * j : 256 * j + 256, :] = dot_tn(cov[:32], pick).astype(BF)
    marks = marks_ref[...].astype(F32)
    mmsg[...] = jnp.concatenate([marks, jnp.zeros((SQ, 128 - CB), F32)], axis=1).astype(BF)
    for j in range(CB):
        g, b = j // 8, j % 8
        m = jnp.broadcast_to(marks[:, j : j + 1], (SQ, 128))
        lhs_r[16 * g : 16 * g + 16, 256 * b : 256 * b + 128] = (zs0[pl.ds(j, SQ, stride=CB), :] * m).astype(BF)
        lhs_r[16 * g : 16 * g + 16, 256 * b + 128 : 256 * b + 256] = (
            zs1[pl.ds(j, SQ, stride=CB), :] * m
        ).astype(BF)
    y = dot(lhs_r[...], wbd_r[...]).astype(BF)
    for g in range(11):
        rmsg[:, 256 * g : 256 * g + 256] = y[16 * g : 16 * g + 16]
    for b in range(2):
        y = dot(lhs_r[:, 1024 * b : 1024 * b + 1024], wbd_l[...]).astype(BF)
        for jg in range(11):
            g = 2 * jg + b
            lmsg[g // 11, :, 128 * (g % 11) : 128 * (g % 11) + 128] = y[16 * jg : 16 * jg + 16]
    rmsg[:, 2816:] = mmsg[...]
    for h in range(2):
        part = [marks[:, RB * h : RB * h + RB], jnp.zeros((SQ, 128 - RB), F32)]
        lmsg[h, :, 1408:] = jnp.concatenate(part, axis=1).astype(BF)

    pl.semaphore_wait(bar, ND - 1)

    keep(rmsg, rall.at[r], S_R)
    for k in range(2, NR, 2):
        send(rmsg, rall.at[r], S_R, r ^ k, c)
    send(rmsg, rall.at[r], S_R2, r ^ 1, c)
    for h in range(2):
        for b in range(NC):
            here = jnp.logical_and(own, jnp.logical_and(r % 2 == h, c == b))

            @pl.when(here)
            def _():
                keep(lmsg.at[h], lall.at[r], S_L)

            @pl.when(jnp.logical_not(here))
            def _():
                send(lmsg.at[h], lall.at[r], S_L, 2 * c + h, jnp.int32(b))

    scale = LOG2E / math.sqrt(32.0)

    w_wide = []
    for h in range(8):
        w_wide += [w_gate[:, 32 * h : 32 * h + 32]] * 4
    w_wide = jnp.concatenate(w_wide, axis=1)
    wide_group = iota((CB, 1024), 1) % 128 // 32

    def project(sg):
        ys = []
        gate = None
        for t in range(4):
            v = zb[4 * sg + t]
            kv = dot(v, w_kv[...])
            ys.append((dot(v, w_q[...]) * scale, kv[:, :256], kv[:, 256:]))
            y = dot(v, w_wide)
            gate = y if gate is None else jnp.where(wide_group == t, y, gate)
        gates[sg] = jax.nn.sigmoid(gate)
        for kind in range(3):
            for h in range(8):
                piece = jnp.concatenate([y[kind][:, 32 * h : 32 * h + 32] for y in ys], axis=1)
                qmsg[h, sg, :, 128 * kind : 128 * kind + 128] = piece.astype(BF)

    loop(0, 4, project)

    bd[...] = jnp.zeros_like(bd)
    st[0:1024, :] = w_opm[...].astype(F32)
    for e in range(32):
        w_opm_e[e] = st[pl.ds(e, 32, stride=32), :].astype(BF)

    arrived(rall.at[pl.ds(0, 8)], S_R)
    for k in range(2, NR, 2):
        send(rall.at[r ^ k], rall.at[r ^ k], S_R2, r ^ 1, c)
    arrived(lall, S_L)
    arrived(rall.at[pl.ds(0, 8)], S_R2)

    keep(qmsg.at[c], qrecv.at[c], S_QK)
    keep(mmsg, mrecv.at[c], S_MK)
    for k in range(1, NC):
        send(mmsg, mrecv.at[c], S_MK, r, c ^ k)
        send(qmsg.at[c ^ k], qrecv.at[c], S_QK, r, c ^ k)

    for g in range(22):
        rt[128 * g : 128 * g + 128, :] = rall[:, :, 128 * g : 128 * g + 128].reshape(256, 128).T
    counts = dot_tn(
        rall[:, :, 2816:].reshape(256, 128), lall[:, :, 1408:].reshape(256, 128)
    ).astype(BF)
    for ig in range(6):
        lhs = lall[:, :, 256 * ig : 256 * ig + 256].reshape(256, 256)
        for part in range(4):
            at = slice(N * part, N * part + N)
            xs[at, :] = dot(rt[at, :], lhs)

        def regroup(e):
            rows = [xs[pl.ds(pl.multiple_of(256 * g + 8 * e, 8), 8), :] for g in range(11)]
            rows.append(jnp.zeros((8, 256), F32))
            xb[e, 96 * ig : 96 * ig + 96, :] = jnp.concatenate(rows, axis=0).astype(BF)

        loop(0, 32, regroup)

    for ec in range(4):
        for e in range(8):
            for i in range(8):
                bd[256 * e + 32 * i : 256 * e + 32 * i + 32, 128 * i : 128 * i + 128] = w_opm_e[8 * ec + e]
        for part in range(3):
            at = slice(192 * part, 192 * part + 192)
            lhs = jnp.concatenate([xb[8 * ec + e, at, :] for e in range(8)], axis=1)
            for n in range(4):
                y = dot(lhs, bd[:, 256 * n : 256 * n + 256])
                if ec:
                    acc_ref[at, 256 * n : 256 * n + 256] += y
                else:
                    acc_ref[at, 256 * n : 256 * n + 256] = y

    code = code_col[...]
    ordinals, strands = code % 4096, code // 4096 % 16
    lane = iota((CB, 128), 1)
    kind = iota((CB, dist_ref.shape[0]), 1)
    ordinals, strands = ordinals[:, : kind.shape[1]], strands[:, : kind.shape[1]]
    fill = jnp.zeros((128 - CB, 128), F32)

    def wide(v):
        return jnp.concatenate([v, fill], axis=0).astype(BF)

    def pair_rows(ig, number):
        pick = (iota((128, 1024), 0) == 8 * ig + iota((128, 1024), 1) // 128).astype(BF)
        weight = 1.0 / (count_eps + dot(counts, pick)[:CB])
        rows = pl.ds(pl.multiple_of(96 * ig, 8), CB)
        for b in range(number):
            i = 8 * ig + b
            row_code = code_ref[r * RB + i]
            bins = jnp.clip(row_code % 4096 - ordinals + REL_MAX, 0, 2 * REL_MAX)
            bins = jnp.where(strands == row_code // 4096 % 16, bins, 2 * REL_MAX + 1)
            z = pair_ref[i].astype(F32) + dot((bins == kind).astype(BF), dist_ref[...])
            z = z + acc_ref[rows, 128 * b : 128 * b + 128] * weight[:, 128 * b : 128 * b + 128]
            zscr[i] = z
            v = norm(z)
            high = wide(v)
            low = (jnp.concatenate([v, fill], axis=0) - high.astype(F32)).astype(BF)
            hb[i] = high
            bias = dot_nt(w_all[512:528, :], high) + dot_nt(w_all[512:528, :], low)
            st_b[pl.ds(i, 8, stride=RP), :] = bias[:8] * LOG2E

    loop(0, 5, lambda ig: pair_rows(ig, 8))
    pair_rows(5, 4)

    def packed(ref, first):
        return pack([ref[pl.ds(pl.multiple_of(first + 8 * k, 8), 8), :] for k in range(6)]).astype(BF)

    for h in range(8):
        bmsg[h] = packed(st_b, RP * h)
    keep(bmsg.at[c], brecv.at[me], S_B)

    @pl.loop(1, ND // 2)
    def _(k):
        rr, cc = r ^ (k // NC * 2), c ^ (k % NC)
        send(bmsg.at[cc], brecv.at[me], S_B, rr, cc)

    live = jnp.concatenate([(code // 65536).astype(F32), fill], axis=0).T[:1]

    def tri_side(base, msg, recv, sem):
        def tri_rows(i):
            y = dot_nt(w_all[base : base + 256, :], hb[i])
            alive = live * (code_ref[r * RB + i] // 65536).astype(F32)
            st[pl.ds(i, 128, stride=RP), :] = jax.nn.sigmoid(y[128:]) * y[:128] * alive

        loop(0, RB, tri_rows, 2)

        def tri_pack(ch):
            msg[ch] = packed(st, RP * ch)

        loop(0, ND, tri_pack, 4)
        keep(msg.at[me], recv.at[me], sem)

        @pl.loop(1, ND)
        def _(k):
            rr, cc = r ^ (k // NC), c ^ (k % NC)
            send(msg.at[rr * NC + cc], recv.at[me], sem, rr, cc)

    tri_side(0, tl_msg, tl_recv, S_TL)

    arrived(brecv.at[pl.ds(0, ND // 2)], S_B)
    for k in range(0, NR, 2):
        at = pl.ds((r ^ k) * NC, NC)
        send(brecv.at[at], brecv.at[at], S_B2, r ^ 1, c)

    tri_side(256, tr_msg, tr_recv, S_TR)

    arrived(qrecv, S_QK)
    arrived(mrecv, S_MK)

    def gather_keys(sg):
        for b in range(NC):
            kf[CB * b : CB * b + CB, :] = qrecv[b, sg, :, 128:256].astype(F32)
        kb[sg] = kf[...].astype(BF)
        for b in range(NC):
            kf[CB * b : CB * b + CB, :] = qrecv[b, sg, :, 256:384].astype(F32)
        vb[sg, :, :128] = kf[...].astype(BF)
        vb[sg, :, 128:] = jnp.ones((N, 128), BF)

    loop(0, 4, gather_keys)
    every = jnp.concatenate([mrecv[b].astype(F32)[:, :CB] for b in range(NC)], axis=1)
    madd = jnp.where(every > 0, 0.0, masked_score)
    group = lane // 32
    arrived(brecv.at[pl.ds(0, ND // 2)], S_B2)

    def attend(k):
        cb = c ^ k
        halves = []
        for d in range(2):
            row = [
                jnp.concatenate(unpack(brecv[(2 * cb + d) * NC + b].astype(F32)), axis=0)[:RB, :CB]
                for b in range(NC)
            ]
            halves.append(jnp.concatenate(row, axis=1))
        biasbuf[...] = jnp.concatenate(halves, axis=0)
        for sg in range(4):
            own_q = qrecv[cb, sg].astype(F32)
            q = jnp.concatenate([jnp.where(group == t, own_q[:, :128], 0.0) for t in range(4)], axis=0)
            s = dot_nt(q.astype(BF), kb[sg])
            ps = []
            for t in range(4):
                v = s[CB * t : CB * t + CB] + biasbuf[...] + madd[4 * sg + t : 4 * sg + t + 1]
                ps.append(jnp.exp2(v - jnp.max(v, axis=-1, keepdims=True)))
            o = dot(jnp.concatenate(ps, axis=0).astype(BF), vb[sg])
            o = o[:, :128] / o[:, 128:]
            mixed = o[:CB]
            for t in range(1, 4):
                mixed = jnp.where(group == t, o[CB * t : CB * t + CB], mixed)
            gmsg[cb, sg] = mixed.astype(BF)

        @pl.when(k == 0)
        def _():
            keep(gmsg.at[c], grecv.at[c], S_G)

        @pl.when(k > 0)
        def _():
            send(gmsg.at[cb], grecv.at[c], S_G, r, cb)

    loop(0, NC, attend)

    def unpack_side(recv, buf):
        def step(q):
            for b in range(NC):
                tile = jnp.concatenate(unpack(recv[q * NC + b].astype(F32)), axis=0).astype(BF)
                buf[b // 2, pl.ds(pl.multiple_of(RP * q, 16), RP), 128 * (b % 2) : 128 * (b % 2) + 128] = tile

        loop(0, NR, step)

    arrived(tl_recv, S_TL)
    unpack_side(tl_recv, lbuf)
    arrived(tr_recv, S_TR)
    unpack_side(tr_recv, rbuf)
    for pair in range(4):
        total = None
        for b in range(4):
            y = dot_nt(lbuf[b], rbuf[b, 4 * RP * pair : 4 * RP * pair + 4 * RP, :])
            total = y if total is None else total + y
        for h in range(2):
            at = 96 * h
            pbuf[...] = jnp.concatenate(
                [total[:, at : at + RB], total[:, at + RP : at + RP + RB], jnp.zeros((NR * RP, 128 - CB), F32)],
                axis=1,
            )

            def cross_pack(q):
                tout[q * NC + 2 * pair + h] = packed(pbuf, RP * q)

            loop(0, NR, cross_pack, 4)

        @pl.loop(0, 2 * NR)
        def _(k):
            rr, cc = r ^ (k // 2), 2 * pair + k % 2
            here = jnp.logical_and(rr == r, cc == c)

            @pl.when(here)
            def _():
                keep(tout.at[me], xrecv.at[me], S_X)

            @pl.when(jnp.logical_not(here))
            def _():
                send(tout.at[rr * NC + cc], xrecv.at[me], S_X, rr, cc)

    arrived(grecv, S_G)
    w_rep = []
    for h in range(8):
        w_rep += [w_mix[32 * h : 32 * h + 32, :]] * 4
    w_rep = jnp.concatenate(w_rep, axis=0)

    def mix(sg):
        cat = jnp.concatenate([grecv[h, sg].astype(F32) for h in range(8)], axis=1) * gates[sg]
        for t in range(4):
            y = dot(jnp.where(wide_group == t, cat, 0.0).astype(BF), w_rep)
            out_a[4 * sg + t] = (x_ref[4 * sg + t].astype(F32) + y).astype(BF)

    loop(0, 4, mix)

    arrived(xrecv, S_X)

    def add(ch, t):
        u = jnp.concatenate(unpack(xrecv[ch].astype(F32)), axis=0)
        st[pl.ds(pl.multiple_of(RP * ch, 8), RP), :] = u
        return t + u

    mean = lax.fori_loop(0, ND, add, jnp.zeros((RP, 128), F32), unroll=4) * (1.0 / 128)

    def square(ch, t):
        d = st[pl.ds(pl.multiple_of(RP * ch, 8), RP), :] - mean
        return t + d * d

    total = lax.fori_loop(0, ND, square, jnp.zeros((RP, 128), F32), unroll=4)
    stats[0:RP, :] = mean
    stats[RP:, :] = lax.rsqrt(total * (1.0 / 128) + norm_eps)

    def last(i):
        cross = (st[pl.ds(i, 128, stride=RP), :] - stats[pl.ds(i, 1), :]) * stats[pl.ds(RP + i, 1), :]
        proj = dot_tn(cross.astype(BF), w_exit[...])[:CB]
        gate = jax.nn.sigmoid(dot(hb[i], w_valve[...])[:CB])
        out_b[i] = (zscr[i] + gate * proj).astype(BF)

    loop(0, RB, last, 2)

    sent(rall.at[pl.ds(0, 7)], S_R)
    sent(rall.at[pl.ds(0, 8)], S_R2)

    @pl.when(own)
    def _():
        sent(lall.at[pl.ds(0, NR - 1)], S_L)

    @pl.when(jnp.logical_not(own))
    def _():
        sent(lall, S_L)

    sent(qrecv.at[pl.ds(0, NC - 1)], S_QK)
    sent(mrecv.at[pl.ds(0, NC - 1)], S_MK)
    sent(brecv.at[pl.ds(0, ND // 2 - 1)], S_B)
    sent(brecv.at[pl.ds(0, ND // 2)], S_B2)
    sent(tl_recv.at[pl.ds(0, ND - 1)], S_TL)
    sent(tr_recv.at[pl.ds(0, ND - 1)], S_TR)
    sent(grecv.at[pl.ds(0, NC - 1)], S_G)
    sent(xrecv.at[pl.ds(0, ND - 1)], S_X)


def run(*operands):
    vm = pl.BlockSpec(memory_space=pltpu.VMEM)
    sm = pl.BlockSpec(memory_space=pltpu.SMEM)
    V = pltpu.VMEM
    scratch = [
        V((SQ * CB, 128), F32), V((SQ * CB, 128), F32), V((SQ, CB, 256), BF),
        V((176, 2048), BF), V((2048, 256), BF), V((1024, 128), BF),
        V((528, 128), BF), V((32, 32, 128), BF), V((4, CB, 1024), F32),
        V((SQ, 128), BF), V((SQ, WR), BF), V((2, SQ, WL), BF), V((8, 4, CB, 384), BF),
        V((2048, 1024), BF), V((2816, 256), BF), V((2816, 256), F32),
        V((32, 576, 256), BF), V((576, 1024), F32),
        V((RB, CB, 128), F32), V((RB, 128, 128), BF),
        V((ND * RP, 128), F32), V((8 * RP, 128), F32), V((8, PK, 128), BF),
        V((ND, PK, 128), BF), V((ND, PK, 128), BF),
        V((N, 128), F32), V((4, N, 128), BF), V((4, N, 256), BF), V((CB, N), F32),
        V((NC, 4, CB, 128), BF), V((4, NR * RP, 256), BF), V((4, NR * RP, 256), BF),
        V((NR * RP, 128), F32), V((ND, PK, 128), BF), V((2 * RP, 128), F32),
        V((NR, SQ, WR), BF), V((NR, SQ, WL), BF), V((NC, 4, CB, 384), BF), V((NC, SQ, 128), BF),
        V((ND, PK, 128), BF), V((ND, PK, 128), BF), V((ND, PK, 128), BF), V((NC, 4, CB, 128), BF),
        V((ND, PK, 128), BF),
        pltpu.SemaphoreType.DMA((11,)), pltpu.SemaphoreType.DMA((11,)),
    ]
    return pl.pallas_call(
        kernel,
        out_shape=(
            jax.ShapeDtypeStruct((SQ, CB, 256), BF),
            jax.ShapeDtypeStruct((RB, CB, 128), BF),
        ),
        in_specs=[vm] * 3 + [sm] + [vm] * 12,
        out_specs=(vm, vm),
        scratch_shapes=scratch,
        compiler_params=pltpu.CompilerParams(
            collective_id=0, has_side_effects=True, vmem_limit_bytes=63 << 20
        ),
    )(*operands)


def shards(
    msa, pair, marks, res_marks, ordinals, strand, dist_vectors, w_bias, w_q, w_kv, w_gate, w_mix,
    w_cov, w_opm, w_tri, w_valve, w_exit,
):
    c = lax.axis_index("col")
    code = ordinals + 4096 * strand + 65536 * res_marks
    code_col = jnp.broadcast_to(lax.dynamic_slice_in_dim(code, c * CB, CB)[:, None], (CB, 128))
    return run(
        msa, pair, marks, code, code_col, w_cov.T, w_q, w_kv, w_gate, w_mix, w_opm, dist_vectors,
        w_tri, w_bias.T, w_valve, w_exit,
    )


def solution(mesh):
    placed = (P("row", "col", None), P("row", "col", None), P("row", "col")) + (P(),) * 14
    return jax.shard_map(
        shards,
        mesh=mesh,
        in_specs=placed,
        out_specs=(P("row", "col", None), P("row", "col", None)),
        check_vma=False,
    )
```

```python
import math

import jax
import jax.numpy as jnp
from jax import lax
from jax.experimental import pallas as pl
from jax.experimental.pallas import tpu as pltpu
from jax.sharding import PartitionSpec as P

REL_MAX = 32
norm_eps = 1e-05
count_eps = 0.001
masked_score = -1000000000.0
LOG2E = 1.4426950408889634
MESH = pl.DeviceIdType.MESH
BF = jnp.bfloat16
F32 = jnp.float32

NR, NC = 16, 8
ND = NR * NC
SQ, RB, CB = 16, 44, 88
N = 704
RP = 48
WR = 2816 + 128
WL = 1408 + 128
S_R, S_R2, S_L, S_QK, S_MK, S_B, S_B2, S_TL, S_TR, S_G, S_X = range(11)
PK = 32


def norm(v):
    v = v.astype(F32)
    v = v - jnp.mean(v, axis=-1, keepdims=True)
    return v * lax.rsqrt(jnp.mean(v * v, axis=-1, keepdims=True) + norm_eps)


def dot(a, b):
    return jnp.dot(a, b, preferred_element_type=F32)


def dot_nt(a, b):
    return lax.dot_general(a, b, (((1,), (1,)), ((), ())), preferred_element_type=F32)


def dot_tn(a, b):
    return lax.dot_general(a, b, (((0,), (0,)), ((), ())), preferred_element_type=F32)


def iota(shape, dim):
    return lax.broadcasted_iota(jnp.int32, shape, dim)


def loop(low, high, body, unroll=1):
    def step(k, carry):
        body(k)
        return carry

    lax.fori_loop(low, high, step, 0, unroll=unroll)


def roll(v, lanes):
    return pltpu.roll(v, lanes, 1)


def pack(u):
    lane, sub = iota((8, 128), 1), iota((8, 128), 0)
    extra = (
        roll(u[4], 88),
        roll(u[4], 48),
        jnp.where(sub < 4, roll(u[5], 88), pltpu.roll(roll(u[5], 48), 4, 0)),
        jnp.where(lane < 96, roll(u[4], 8), roll(u[5], 16)),
    )
    return jnp.concatenate([jnp.where(lane < CB, u[k], extra[k]) for k in range(4)], axis=0)


def unpack(p):
    lane = iota((8, 128), 1)
    p = [p[8 * k : 8 * k + 8] for k in range(4)]
    low, mid, high = lane < 40, lane < 80, lane < CB
    u = [jnp.where(high, v, 0.0) for v in p]
    tail = jnp.where(high, roll(p[3], 120), 0.0)
    u.append(jnp.where(low, roll(p[0], 40), jnp.where(mid, roll(p[1], 80), tail)))
    tail = jnp.where(high, roll(p[3], 112), 0.0)
    u.append(jnp.where(low, roll(p[2], 40), jnp.where(mid, pltpu.roll(roll(p[2], 80), 4, 0), tail)))
    return u


def kernel(
    x_ref, pair_ref, marks_ref, code_ref, code_col, w_cov, w_q, w_kv, w_gate, w_mix,
    w_opm, dist_ref, w_tri, w_bias, w_valve, w_exit,
    out_a, out_b,
    zs0, zs1, zb, lhs_r, wbd_r, wbd_l, w_all, w_opm_e, gates, mmsg, rmsg, lmsg, qmsg, bd, rt, xs, xb, acc_ref,
    zscr, hb, st, st_b, bmsg, tl_msg, tr_msg, kf, kb, vb, biasbuf, gmsg, lbuf, rbuf, pbuf, tout, stats,
    rall, lall, qrecv, mrecv, brecv, tl_recv, tr_recv, grecv, xrecv,
    ssem, rsem,
):
    r = lax.axis_index("row")
    c = lax.axis_index("col")
    me = r * NC + c
    own = (r // 2) == c

    def send(src, dst, kind, rr, cc):
        pltpu.make_async_remote_copy(
            src, dst, ssem.at[kind], rsem.at[kind], device_id=(rr, cc), device_id_type=MESH
        ).start()

    def keep(src, dst, kind):
        pltpu.make_async_copy(src, dst, rsem.at[kind]).start()

    def arrived(ref, kind):
        pltpu.make_async_copy(ref, ref, rsem.at[kind]).wait()

    def sent(ref, kind):
        pltpu.make_async_copy(ref, ref, ssem.at[kind]).wait()

    bar = pltpu.get_barrier_semaphore()

    @pl.loop(1, ND)
    def _(k):
        pl.semaphore_signal(bar, inc=1, device_id=(r ^ (k // NC), c ^ (k % NC)), device_id_type=MESH)

    for k in range(4):
        w_all[128 * k : 128 * k + 128, :] = w_tri[:, 128 * k : 128 * k + 128].T
    w_all[512:, :] = jnp.concatenate([w_bias[...].astype(F32), jnp.zeros((8, 128), F32)], axis=0).astype(BF)

    def msa_norm(s):
        v = norm(x_ref[s])
        at = pl.ds(pl.multiple_of(s * CB, 8), CB)
        zs0[at, :] = v[:, :128]
        zs1[at, :] = v[:, 128:]
        zb[s] = v.astype(BF)

    loop(0, SQ, msa_norm)

    cov = w_cov[...]
    for j in range(8):
        pick = (iota((32, 256), 1) == 8 * iota((32, 256), 0) + j).astype(BF)
        wbd_r[256 * j : 256 * j + 256, :] = dot_tn(cov[32:], pick).astype(BF)
    for j in range(4):
        pick = (iota((32, 128), 1) == 32 * j + iota((32, 128), 0)).astype(BF)
        wbd_l[256 * j : 256 * j + 256, :] = dot_tn(cov[:32], pick).astype(BF)
    marks = marks_ref[...].astype(F32)
    mmsg[...] = jnp.concatenate([marks, jnp.zeros((SQ, 128 - CB), F32)], axis=1).astype(BF)
    for j in range(CB):
        g, b = j // 8, j % 8
        m = jnp.broadcast_to(marks[:, j : j + 1], (SQ, 128))
        lhs_r[16 * g : 16 * g + 16, 256 * b : 256 * b + 128] = (zs0[pl.ds(j, SQ, stride=CB), :] * m).astype(BF)
        lhs_r[16 * g : 16 * g + 16, 256 * b + 128 : 256 * b + 256] = (
            zs1[pl.ds(j, SQ, stride=CB), :] * m
        ).astype(BF)
    y = dot(lhs_r[...], wbd_r[...]).astype(BF)
    for g in range(11):
        rmsg[:, 256 * g : 256 * g + 256] = y[16 * g : 16 * g + 16]
    for b in range(2):
        y = dot(lhs_r[:, 1024 * b : 1024 * b + 1024], wbd_l[...]).astype(BF)
        for jg in range(11):
            g = 2 * jg + b
            lmsg[g // 11, :, 128 * (g % 11) : 128 * (g % 11) + 128] = y[16 * jg : 16 * jg + 16]
    rmsg[:, 2816:] = mmsg[...]
    for h in range(2):
        part = [marks[:, RB * h : RB * h + RB], jnp.zeros((SQ, 128 - RB), F32)]
        lmsg[h, :, 1408:] = jnp.concatenate(part, axis=1).astype(BF)

    pl.semaphore_wait(bar, ND - 1)

    keep(rmsg, rall.at[r], S_R)
    for k in range(2, NR, 2):
        send(rmsg, rall.at[r], S_R, r ^ k, c)
    send(rmsg, rall.at[r], S_R2, r ^ 1, c)
    for h in range(2):
        for b in range(NC):
            here = jnp.logical_and(own, jnp.logical_and(r % 2 == h, c == b))

            @pl.when(here)
            def _():
                keep(lmsg.at[h], lall.at[r], S_L)

            @pl.when(jnp.logical_not(here))
            def _():
                send(lmsg.at[h], lall.at[r], S_L, 2 * c + h, jnp.int32(b))

    scale = LOG2E / math.sqrt(32.0)

    w_wide = []
    for h in range(8):
        w_wide += [w_gate[:, 32 * h : 32 * h + 32]] * 4
    w_wide = jnp.concatenate(w_wide, axis=1)
    wide_group = iota((CB, 1024), 1) % 128 // 32

    def project(sg):
        ys = []
        gate = None
        for t in range(4):
            v = zb[4 * sg + t]
            kv = dot(v, w_kv[...])
            ys.append((dot(v, w_q[...]) * scale, kv[:, :256], kv[:, 256:]))
            y = dot(v, w_wide)
            gate = y if gate is None else jnp.where(wide_group == t, y, gate)
        gates[sg] = jax.nn.sigmoid(gate)
        for kind in range(3):
            for h in range(8):
                piece = jnp.concatenate([y[kind][:, 32 * h : 32 * h + 32] for y in ys], axis=1)
                qmsg[h, sg, :, 128 * kind : 128 * kind + 128] = piece.astype(BF)

    loop(0, 4, project)

    bd[...] = jnp.zeros_like(bd)
    st[0:1024, :] = w_opm[...].astype(F32)
    for e in range(32):
        w_opm_e[e] = st[pl.ds(e, 32, stride=32), :].astype(BF)

    arrived(rall.at[pl.ds(0, 8)], S_R)
    for k in range(2, NR, 2):
        send(rall.at[r ^ k], rall.at[r ^ k], S_R2, r ^ 1, c)
    arrived(lall, S_L)
    arrived(rall.at[pl.ds(0, 8)], S_R2)

    keep(qmsg.at[c], qrecv.at[c], S_QK)
    keep(mmsg, mrecv.at[c], S_MK)
    for k in range(1, NC):
        send(mmsg, mrecv.at[c], S_MK, r, c ^ k)
        send(qmsg.at[c ^ k], qrecv.at[c], S_QK, r, c ^ k)

    for g in range(22):
        rt[128 * g : 128 * g + 128, :] = rall[:, :, 128 * g : 128 * g + 128].reshape(256, 128).T
    counts = dot_tn(
        rall[:, :, 2816:].reshape(256, 128), lall[:, :, 1408:].reshape(256, 128)
    ).astype(BF)
    for ig in range(6):
        lhs = lall[:, :, 256 * ig : 256 * ig + 256].reshape(256, 256)
        for part in range(4):
            at = slice(N * part, N * part + N)
            xs[at, :] = dot(rt[at, :], lhs)

        def regroup(e):
            rows = [xs[pl.ds(pl.multiple_of(256 * g + 8 * e, 8), 8), :] for g in range(11)]
            rows.append(jnp.zeros((8, 256), F32))
            xb[e, 96 * ig : 96 * ig + 96, :] = jnp.concatenate(rows, axis=0).astype(BF)

        loop(0, 32, regroup)

    for ec in range(4):
        for e in range(8):
            for i in range(8):
                bd[256 * e + 32 * i : 256 * e + 32 * i + 32, 128 * i : 128 * i + 128] = w_opm_e[8 * ec + e]
        for part in range(3):
            at = slice(192 * part, 192 * part + 192)
            lhs = jnp.concatenate([xb[8 * ec + e, at, :] for e in range(8)], axis=1)
            for n in range(4):
                y = dot(lhs, bd[:, 256 * n : 256 * n + 256])
                if ec:
                    acc_ref[at, 256 * n : 256 * n + 256] += y
                else:
                    acc_ref[at, 256 * n : 256 * n + 256] = y

    code = code_col[...]
    ordinals, strands = code % 4096, code // 4096 % 16
    lane = iota((CB, 128), 1)
    kind = iota((CB, dist_ref.shape[0]), 1)
    ordinals, strands = ordinals[:, : kind.shape[1]], strands[:, : kind.shape[1]]
    fill = jnp.zeros((128 - CB, 128), F32)

    def wide(v):
        return jnp.concatenate([v, fill], axis=0).astype(BF)

    def pair_rows(ig, number):
        pick = (iota((128, 1024), 0) == 8 * ig + iota((128, 1024), 1) // 128).astype(BF)
        weight = 1.0 / (count_eps + dot(counts, pick)[:CB])
        rows = pl.ds(pl.multiple_of(96 * ig, 8), CB)
        for b in range(number):
            i = 8 * ig + b
            row_code = code_ref[r * RB + i]
            bins = jnp.clip(row_code % 4096 - ordinals + REL_MAX, 0, 2 * REL_MAX)
            bins = jnp.where(strands == row_code // 4096 % 16, bins, 2 * REL_MAX + 1)
            z = pair_ref[i].astype(F32) + dot((bins == kind).astype(BF), dist_ref[...])
            z = z + acc_ref[rows, 128 * b : 128 * b + 128] * weight[:, 128 * b : 128 * b + 128]
            zscr[i] = z
            v = norm(z)
            high = wide(v)
            low = (jnp.concatenate([v, fill], axis=0) - high.astype(F32)).astype(BF)
            hb[i] = high
            bias = dot_nt(w_all[512:528, :], high) + dot_nt(w_all[512:528, :], low)
            st_b[pl.ds(i, 8, stride=RP), :] = bias[:8] * LOG2E

    loop(0, 5, lambda ig: pair_rows(ig, 8))
    pair_rows(5, 4)

    def packed(ref, first):
        return pack([ref[pl.ds(pl.multiple_of(first + 8 * k, 8), 8), :] for k in range(6)]).astype(BF)

    for h in range(8):
        bmsg[h] = packed(st_b, RP * h)
    keep(bmsg.at[c], brecv.at[me], S_B)

    @pl.loop(1, ND // 2)
    def _(k):
        rr, cc = r ^ (k // NC * 2), c ^ (k % NC)
        send(bmsg.at[cc], brecv.at[me], S_B, rr, cc)

    live = jnp.concatenate([(code // 65536).astype(F32), fill], axis=0).T[:1]

    def tri_side(base, msg, recv, sem):
        def tri_rows(i):
            y = dot_nt(w_all[base : base + 256, :], hb[i])
            alive = live * (code_ref[r * RB + i] // 65536).astype(F32)
            st[pl.ds(i, 128, stride=RP), :] = jax.nn.sigmoid(y[128:]) * y[:128] * alive

        loop(0, RB, tri_rows, 2)

        def tri_pack(ch):
            msg[ch] = packed(st, RP * ch)

        loop(0, ND, tri_pack, 4)
        keep(msg.at[me], recv.at[me], sem)

        @pl.loop(1, ND)
        def _(k):
            rr, cc = r ^ (k // NC), c ^ (k % NC)
            send(msg.at[rr * NC + cc], recv.at[me], sem, rr, cc)

    tri_side(0, tl_msg, tl_recv, S_TL)

    arrived(brecv.at[pl.ds(0, ND // 2)], S_B)
    for k in range(0, NR, 2):
        at = pl.ds((r ^ k) * NC, NC)
        send(brecv.at[at], brecv.at[at], S_B2, r ^ 1, c)

    tri_side(256, tr_msg, tr_recv, S_TR)

    arrived(qrecv, S_QK)
    arrived(mrecv, S_MK)

    def gather_keys(sg):
        for b in range(NC):
            kf[CB * b : CB * b + CB, :] = qrecv[b, sg, :, 128:256].astype(F32)
        kb[sg] = kf[...].astype(BF)
        for b in range(NC):
            kf[CB * b : CB * b + CB, :] = qrecv[b, sg, :, 256:384].astype(F32)
        vb[sg, :, :128] = kf[...].astype(BF)
        vb[sg, :, 128:] = jnp.ones((N, 128), BF)

    loop(0, 4, gather_keys)
    every = jnp.concatenate([mrecv[b].astype(F32)[:, :CB] for b in range(NC)], axis=1)
    madd = jnp.where(every > 0, 0.0, masked_score)
    group = lane // 32
    arrived(brecv.at[pl.ds(0, ND // 2)], S_B2)

    def attend(k):
        cb = c ^ k
        halves = []
        for d in range(2):
            row = [
                jnp.concatenate(unpack(brecv[(2 * cb + d) * NC + b].astype(F32)), axis=0)[:RB, :CB]
                for b in range(NC)
            ]
            halves.append(jnp.concatenate(row, axis=1))
        biasbuf[...] = jnp.concatenate(halves, axis=0)
        for sg in range(4):
            own_q = qrecv[cb, sg].astype(F32)
            q = jnp.concatenate([jnp.where(group == t, own_q[:, :128], 0.0) for t in range(4)], axis=0)
            s = dot_nt(q.astype(BF), kb[sg])
            ps = []
            for t in range(4):
                v = s[CB * t : CB * t + CB] + biasbuf[...] + madd[4 * sg + t : 4 * sg + t + 1]
                ps.append(jnp.exp2(v - jnp.max(v, axis=-1, keepdims=True)))
            o = dot(jnp.concatenate(ps, axis=0).astype(BF), vb[sg])
            o = o[:, :128] / o[:, 128:]
            mixed = o[:CB]
            for t in range(1, 4):
                mixed = jnp.where(group == t, o[CB * t : CB * t + CB], mixed)
            gmsg[cb, sg] = mixed.astype(BF)

        @pl.when(k == 0)
        def _():
            keep(gmsg.at[c], grecv.at[c], S_G)

        @pl.when(k > 0)
        def _():
            send(gmsg.at[cb], grecv.at[c], S_G, r, cb)

    loop(0, NC, attend)

    def unpack_side(recv, buf, low, high):
        def step(q):
            for b in range(NC):
                tile = jnp.concatenate(unpack(recv[q * NC + b].astype(F32)), axis=0).astype(BF)
                buf[b // 2, pl.ds(pl.multiple_of(RP * q, 16), RP), 128 * (b % 2) : 128 * (b % 2) + 128] = tile

        loop(low, high, step)

    arrived(tl_recv, S_TL)
    unpack_side(tl_recv, lbuf, 0, NR)
    arrived(tr_recv, S_TR)
    for pair in range(4):
        unpack_side(tr_recv, rbuf, 4 * pair, 4 * pair + 4)
        total = None
        for b in range(4):
            y = dot_nt(lbuf[b], rbuf[b, 4 * RP * pair : 4 * RP * pair + 4 * RP, :])
            total = y if total is None else total + y
        for h in range(2):
            at = 96 * h
            pbuf[...] = jnp.concatenate(
                [total[:, at : at + RB], total[:, at + RP : at + RP + RB], jnp.zeros((NR * RP, 128 - CB), F32)],
                axis=1,
            )

            def cross_pack(q):
                tout[q * NC + 2 * pair + h] = packed(pbuf, RP * q)

            loop(0, NR, cross_pack, 4)

        @pl.loop(0, 2 * NR)
        def _(k):
            rr, cc = r ^ (k // 2), 2 * pair + k % 2
            here = jnp.logical_and(rr == r, cc == c)

            @pl.when(here)
            def _():
                keep(tout.at[me], xrecv.at[me], S_X)

            @pl.when(jnp.logical_not(here))
            def _():
                send(tout.at[rr * NC + cc], xrecv.at[me], S_X, rr, cc)

    def pair_gate(first, lanes):
        def step(k):
            xs[pl.ds(pl.multiple_of(CB * k, 8), CB), lanes : lanes + 128] = jax.nn.sigmoid(
                dot(hb[first + k], w_valve[...])[:CB]
            )

        return step

    loop(0, 32, pair_gate(0, 0), 4)
    loop(0, RB - 32, pair_gate(32, 128), 4)

    arrived(grecv, S_G)
    w_rep = []
    for h in range(8):
        w_rep += [w_mix[32 * h : 32 * h + 32, :]] * 4
    w_rep = jnp.concatenate(w_rep, axis=0)

    def mix(sg):
        cat = jnp.concatenate([grecv[h, sg].astype(F32) for h in range(8)], axis=1) * gates[sg]
        for t in range(4):
            y = dot(jnp.where(wide_group == t, cat, 0.0).astype(BF), w_rep)
            out_a[4 * sg + t] = y

    loop(0, 4, mix)

    arrived(xrecv, S_X)

    def add(ch, t):
        u = jnp.concatenate(unpack(xrecv[ch].astype(F32)), axis=0)
        st[pl.ds(pl.multiple_of(RP * ch, 8), RP), :] = u
        return t + u

    mean = lax.fori_loop(0, ND, add, jnp.zeros((RP, 128), F32), unroll=4) * (1.0 / 128)

    def square(ch, t):
        d = st[pl.ds(pl.multiple_of(RP * ch, 8), RP), :] - mean
        return t + d * d

    total = lax.fori_loop(0, ND, square, jnp.zeros((RP, 128), F32), unroll=4)
    stats[0:RP, :] = mean
    stats[RP:, :] = lax.rsqrt(total * (1.0 / 128) + norm_eps)

    def last(first, lanes):
        def step(k):
            i = first + k
            cross = (st[pl.ds(i, 128, stride=RP), :] - stats[pl.ds(i, 1), :]) * stats[pl.ds(RP + i, 1), :]
            proj = dot_tn(cross.astype(BF), w_exit[...])[:CB]
            gate = xs[pl.ds(pl.multiple_of(CB * k, 8), CB), lanes : lanes + 128]
            out_b[i] = (zscr[i] + gate * proj).astype(BF)

        return step

    loop(0, 32, last(0, 0), 4)
    loop(0, RB - 32, last(32, 128), 4)

    sent(rall.at[pl.ds(0, 7)], S_R)
    sent(rall.at[pl.ds(0, 8)], S_R2)

    @pl.when(own)
    def _():
        sent(lall.at[pl.ds(0, NR - 1)], S_L)

    @pl.when(jnp.logical_not(own))
    def _():
        sent(lall, S_L)

    sent(qrecv.at[pl.ds(0, NC - 1)], S_QK)
    sent(mrecv.at[pl.ds(0, NC - 1)], S_MK)
    sent(brecv.at[pl.ds(0, ND // 2 - 1)], S_B)
    sent(brecv.at[pl.ds(0, ND // 2)], S_B2)
    sent(tl_recv.at[pl.ds(0, ND - 1)], S_TL)
    sent(tr_recv.at[pl.ds(0, ND - 1)], S_TR)
    sent(grecv.at[pl.ds(0, NC - 1)], S_G)
    sent(xrecv.at[pl.ds(0, ND - 1)], S_X)


def run(*operands):
    vm = pl.BlockSpec(memory_space=pltpu.VMEM)
    sm = pl.BlockSpec(memory_space=pltpu.SMEM)
    V = pltpu.VMEM
    scratch = [
        V((SQ * CB, 128), F32), V((SQ * CB, 128), F32), V((SQ, CB, 256), BF),
        V((176, 2048), BF), V((2048, 256), BF), V((1024, 128), BF),
        V((528, 128), BF), V((32, 32, 128), BF), V((4, CB, 1024), F32),
        V((SQ, 128), BF), V((SQ, WR), BF), V((2, SQ, WL), BF), V((8, 4, CB, 384), BF),
        V((2048, 1024), BF), V((2816, 256), BF), V((2816, 256), F32),
        V((32, 576, 256), BF), V((576, 1024), F32),
        V((RB, CB, 128), F32), V((RB, 128, 128), BF),
        V((ND * RP, 128), F32), V((8 * RP, 128), F32), V((8, PK, 128), BF),
        V((ND, PK, 128), BF), V((ND, PK, 128), BF),
        V((N, 128), F32), V((4, N, 128), BF), V((4, N, 256), BF), V((CB, N), F32),
        V((NC, 4, CB, 128), BF), V((4, NR * RP, 256), BF), V((4, NR * RP, 256), BF),
        V((NR * RP, 128), F32), V((ND, PK, 128), BF), V((2 * RP, 128), F32),
        V((NR, SQ, WR), BF), V((NR, SQ, WL), BF), V((NC, 4, CB, 384), BF), V((NC, SQ, 128), BF),
        V((ND, PK, 128), BF), V((ND, PK, 128), BF), V((ND, PK, 128), BF), V((NC, 4, CB, 128), BF),
        V((ND, PK, 128), BF),
        pltpu.SemaphoreType.DMA((11,)), pltpu.SemaphoreType.DMA((11,)),
    ]
    return pl.pallas_call(
        kernel,
        out_shape=(
            jax.ShapeDtypeStruct((SQ, CB, 256), F32),
            jax.ShapeDtypeStruct((RB, CB, 128), BF),
        ),
        in_specs=[vm] * 3 + [sm] + [vm] * 12,
        out_specs=(vm, vm),
        scratch_shapes=scratch,
        compiler_params=pltpu.CompilerParams(
            collective_id=0, has_side_effects=True, vmem_limit_bytes=63 << 20
        ),
    )(*operands)


def shards(
    msa, pair, marks, res_marks, ordinals, strand, dist_vectors, w_bias, w_q, w_kv, w_gate, w_mix,
    w_cov, w_opm, w_tri, w_valve, w_exit,
):
    c = lax.axis_index("col")
    code = ordinals + 4096 * strand + 65536 * res_marks
    code_col = jnp.broadcast_to(lax.dynamic_slice_in_dim(code, c * CB, CB)[:, None], (CB, 128))
    change, pair_out = run(
        msa, pair, marks, code, code_col, w_cov.T, w_q, w_kv, w_gate, w_mix, w_opm, dist_vectors,
        w_tri, w_bias.T, w_valve, w_exit,
    )
    return (msa.astype(F32) + change).astype(BF), pair_out


def solution(mesh):
    placed = (P("row", "col", None), P("row", "col", None), P("row", "col")) + (P(),) * 14
    return jax.shard_map(
        shards,
        mesh=mesh,
        in_specs=placed,
        out_specs=(P("row", "col", None), P("row", "col", None)),
        check_vma=False,
    )
```
